512 devices in a mesh: batch: 64 (over z, y), proto: 8 (over x, core).
Axes of the slice: x: 4, y: 4, z: 16, core: 2. Of those that a mesh axis runs over, the one named last changes fastest.
Arguments:
- embeddings: bfloat16 [65536, 256], P('batch'), as said below
- prototypes: bfloat16 [16384, 256], P('proto'), as said below
- partner: int32 [65536], P('batch'), may hold values from 0 to 65535, as said below
Outputs:
- emb_grad: float32 [65536, 256], P('batch')
- proto_grad: float32 [16384, 256], P('proto')
The draws below stay inside these ranges and needn't reach their ends.
Inputs may be any that keep to these rules, and one draw needn't show every extreme that they name: partner[partner[b]] == b for every view b, and partner[b] lies in the aligned block of 1024 views whose block index differs from that of b by 32. `embeddings`: no row is zero. `prototypes`: no row is zero.
All inputs are finite; a program needn't handle non-finite values.
Results may differ from the reference program's by a relative error of at most 0.0016.
Values may be sent and summed in bfloat16 or wider, within the bound.
No kernel may reach another device: no remote copies, remote signals or barrier semaphores. Data moves between devices by JAX's collectives and lax.ppermute only.
A program may use at most 64 MiB of HBM per device.

```python
import math
from functools import partial
import jax
import jax.numpy as jnp
from jax import lax

D = 256
PROTOS = 16384
TOK_DEV = 1024
ITERS = 3
TOKENS = 65536


def shared_direction(key):
    return jax.random.normal(jax.random.fold_in(key, 7), (D,), jnp.float32)


def group_directions(key):
    return jax.random.normal(jax.random.fold_in(key, 11), (16, D), jnp.float32)


def draw_embeddings(key, part):
    direction = shared_direction(key)
    table = group_directions(key)
    noise_key = jax.random.fold_in(key, 1)
    noise = jax.random.normal(noise_key, (TOKENS, D), jnp.float32)
    blocks = TOKENS // TOK_DEV
    block_index = jnp.arange(TOKENS, dtype=jnp.int32) // TOK_DEV
    quarter = jnp.minimum(block_index * 4 // blocks, 3)
    group_index = (jnp.remainder(block_index, 4) * 4 + quarter).astype(jnp.int32)
    group_part = table[group_index]
    position = jnp.arange(TOKENS, dtype=jnp.float32) / TOKENS
    scales = jnp.exp(jax.random.uniform(jax.random.fold_in(key, 3), (TOKENS, 1), jnp.float32, 0.0, math.log(10.0)))
    values = (noise + position[:, None] * direction[None, :] + group_part) * scales / 16.0
    return values.astype(jnp.bfloat16)


def draw_prototypes(key, part):
    direction = shared_direction(key)
    table = group_directions(key)
    noise_key = jax.random.fold_in(key, 2)
    noise = jax.random.normal(noise_key, (PROTOS, D), jnp.float32)
    group_index = jnp.remainder(jnp.arange(PROTOS, dtype=jnp.int32), 16).astype(jnp.int32)
    group_part = table[group_index]
    position = jnp.arange(PROTOS, dtype=jnp.float32) / PROTOS
    scales = jnp.exp(jax.random.uniform(jax.random.fold_in(key, 4), (PROTOS, 1), jnp.float32, 0.0, math.log(4.0)))
    values = (noise + position[:, None] * direction[None, :] + group_part) * scales / 16.0
    return values.astype(jnp.bfloat16)


def draw_partner(key, part):
    blocks = TOKENS // TOK_DEV
    halfway = blocks // 2
    ranking = jax.random.randint(jax.random.fold_in(key, 5), (halfway, TOK_DEV), 0, 1048576) * TOK_DEV
    ranking = ranking + jnp.arange(TOK_DEV, dtype=jnp.int32)[None, :]
    ordering = jnp.argsort(ranking, axis=1).astype(jnp.int32)
    inverse = jnp.argsort(ordering, axis=1).astype(jnp.int32)
    starts = jnp.arange(halfway, dtype=jnp.int32)[:, None] * TOK_DEV
    leading = starts + halfway * TOK_DEV + ordering
    trailing = starts + inverse
    return jnp.concatenate([leading.reshape(-1), trailing.reshape(-1)]).astype(jnp.int32)


def setup_inputs(seed: int = 0) -> dict:
    arg_keys = jax.random.split(jax.random.key(seed), 4)
    embeddings = draw_embeddings(jax.random.fold_in(arg_keys[3], 71), 0)
    prototypes = draw_prototypes(jax.random.fold_in(arg_keys[3], 71), 0)
    partner = draw_partner(jax.random.fold_in(arg_keys[3], 71), 0)
    return dict(embeddings=embeddings, prototypes=prototypes, partner=partner)


epsilon_code = 0.05
sharpness_divisor = 0.1
norm_floor = 1e-06

def unit_rows(values):
    wide = values.astype(jnp.float32)
    scale = lax.rsqrt(lax.optimization_barrier(jnp.mean(wide * wide, axis=1, keepdims=True)) + norm_floor) / jnp.sqrt(jnp.float32(wide.shape[1]))
    return (wide * scale, scale)

def norm_back(upstream, units, scale):
    return scale * (upstream - units * lax.optimization_barrier(jnp.sum(units * upstream, axis=1, keepdims=True)))

def contract_rows(left, right):
    return lax.dot_general(left, right, (((0,), (0,)), ((), ())), preferred_element_type=jnp.float32)

def reference(embeddings, prototypes, partner):
    view_units, view_scale = unit_rows(embeddings)
    proto_units, proto_scale = unit_rows(prototypes)
    views = view_units.astype(jnp.bfloat16)
    protos = proto_units.astype(jnp.bfloat16)
    blocks = TOKENS // TOK_DEV
    halfway = blocks // 2
    view_blocks = views.reshape(blocks, TOK_DEV, D)

    def scores_of(block_rows):
        return jnp.dot(block_rows, protos.T, preferred_element_type=jnp.float32)

    def first_step(total, block_rows):
        kernel = jnp.exp(scores_of(block_rows) / epsilon_code)
        return (total + lax.optimization_barrier(jnp.sum(kernel, axis=0)), None)

    def merged_step(column_scale, total, block_rows):
        kernel = jnp.exp(scores_of(block_rows) / epsilon_code)
        weight = 1.0 / lax.optimization_barrier(jnp.sum(kernel * column_scale[None, :], axis=1))
        return (total + lax.optimization_barrier(jnp.sum(weight[:, None] * kernel, axis=0)), None)
    empty = jnp.zeros((PROTOS,), jnp.float32)
    column_total, _ = lax.scan(first_step, empty, view_blocks)
    for sweep in range(ITERS - 1):
        column_scale = 1.0 / column_total
        column_total, _ = lax.scan(partial(merged_step, column_scale), empty, view_blocks)
    column_scale = 1.0 / column_total

    def codes_probs(block_rows):
        centroid_raw_affinities = scores_of(block_rows)
        dispersion_width = jnp.exp(centroid_raw_affinities / epsilon_code) * column_scale[None, :]
        balanced_transport_labels = (dispersion_width * (1.0 / lax.optimization_barrier(jnp.sum(dispersion_width, axis=1)))[:, None]).astype(jnp.bfloat16)
        tempered_affinities = jnp.exp(centroid_raw_affinities / sharpness_divisor)
        estimated_likelihood = tempered_affinities * (1.0 / lax.optimization_barrier(jnp.sum(tempered_affinities, axis=1)))[:, None]
        return (balanced_transport_labels, estimated_likelihood)

    def loss_derivative(estimated_likelihood, balanced_transport_labels):
        return ((estimated_likelihood - balanced_transport_labels.astype(jnp.float32)) / sharpness_divisor).astype(jnp.bfloat16)
    pair_views = view_blocks.reshape(2, halfway, TOK_DEV, D)
    pair_links = jnp.remainder(partner, TOK_DEV).astype(jnp.int32).reshape(2, halfway, TOK_DEV)

    def pair_step(total, item):
        first_rows, second_rows, first_links, second_links = item
        first_codes, first_prob = codes_probs(first_rows)
        second_codes, second_prob = codes_probs(second_rows)
        first_grad = loss_derivative(first_prob, second_codes[first_links])
        second_grad = loss_derivative(second_prob, first_codes[second_links])
        total = total + contract_rows(first_grad, first_rows) + contract_rows(second_grad, second_rows)
        first_up = jnp.dot(first_grad, protos, preferred_element_type=jnp.float32)
        second_up = jnp.dot(second_grad, protos, preferred_element_type=jnp.float32)
        return (total, (first_up, second_up))
    proto_upstream, (first_ups, second_ups) = lax.scan(pair_step, jnp.zeros((PROTOS, D), jnp.float32), (pair_views[0], pair_views[1], pair_links[0], pair_links[1]))
    view_upstream = jnp.concatenate([first_ups.reshape(-1, D), second_ups.reshape(-1, D)], axis=0)
    return (norm_back(view_upstream, view_units, view_scale), norm_back(proto_upstream, proto_units, proto_scale))
```

```python
import jax
import jax.numpy as jnp
from jax import lax
from jax.sharding import Mesh, PartitionSpec as P

ITERS = 3


epsilon_code = 0.05
sharpness_divisor = 0.1
norm_floor = 1e-06
rows_axes = ("z", "y")
proto_axes = ("x", "core")


def shifted(value, axis, steps):
    count = lax.axis_size(axis)
    pairs = [(source, (source + steps) % count) for source in range(count)]
    return lax.ppermute(value, axis, pairs)


def gathered(value, axis):
    count = lax.axis_size(axis)
    copies = jnp.broadcast_to(value[None], (count,) + value.shape)
    return lax.all_to_all(copies, axis, 0, 0, tiled=True)


def unit_rows(values):
    wide = values.astype(jnp.float32)
    scale = lax.rsqrt(jnp.mean(wide * wide, axis=1, keepdims=True) + norm_floor) / jnp.sqrt(
        jnp.float32(wide.shape[1])
    )
    return (wide * scale, scale)


def norm_back(upstream, units, scale):
    return scale * (upstream - units * jnp.sum(units * upstream, axis=1, keepdims=True))


def block(value, index, count):
    size = value.shape[0] // count
    return lax.dynamic_slice_in_dim(value, index * size, size, 0)


def scatter_sum(value, axis):
    count = lax.axis_size(axis)
    me = lax.axis_index(axis)
    total = block(value, me, count)
    for step in range(1, count):
        total = total + shifted(block(value, (me + step) % count, count), axis, step)
    return total


def gather_blocks(value, axis):
    count = lax.axis_size(axis)
    me = lax.axis_index(axis)
    pieces = [value] + [shifted(value, axis, step) for step in range(1, count)]
    out = jnp.zeros((count,) + value.shape, value.dtype)
    for step, piece in enumerate(pieces):
        out = lax.dynamic_update_slice_in_dim(out, piece[None], (me + count - step) % count, 0)
    return out.reshape((-1,) + value.shape[1:])


def contract_rows(left, right):
    return lax.dot_general(
        left, right, (((0,), (0,)), ((), ())), preferred_element_type=jnp.float32
    )


def column_scale_of(part):
    part = lax.psum(part, "y")
    return 1.0 / jnp.sum(gathered(part, "z"), axis=0)


def row_totals(*parts):
    stacked = jnp.concatenate(parts)
    total = jnp.sum(gathered(stacked, proto_axes), axis=0)
    return jnp.split(total, len(parts))


def body(embeddings, prototypes, partner):
    view_units, view_scale = unit_rows(embeddings)
    proto_units, proto_scale = unit_rows(prototypes)
    views = view_units.astype(jnp.bfloat16)
    protos = proto_units.astype(jnp.bfloat16)
    row_count = views.shape[0]
    links = jnp.remainder(partner, row_count)
    other = shifted(embeddings, "z", lax.axis_size("z") // 2)[links]
    other_views = unit_rows(other)[0].astype(jnp.bfloat16)

    scores = jnp.dot(views, protos.T, preferred_element_type=jnp.float32)
    tempered = jnp.exp(scores / sharpness_divisor)
    kernel = tempered * tempered
    soft_part = jnp.sum(tempered, axis=1)
    column_scale = column_scale_of(jnp.sum(kernel, axis=0))
    other_scores = jnp.dot(other_views, protos.T, preferred_element_type=jnp.float32)
    other_kernel = jnp.exp(other_scores / epsilon_code)
    for sweep in range(ITERS - 1):
        row_part = jnp.sum(kernel * column_scale[None, :], axis=1)
        if sweep == 0:
            row_total, soft_total = row_totals(row_part, soft_part)
        else:
            (row_total,) = row_totals(row_part)
        weight = 1.0 / row_total
        column_scale = column_scale_of(jnp.sum(weight[:, None] * kernel, axis=0))
    dispersion = other_kernel * column_scale[None, :]
    (line_total,) = row_totals(jnp.sum(dispersion, axis=1))
    codes = (dispersion * (1.0 / line_total)[:, None]).astype(jnp.bfloat16)
    likelihood = tempered * (1.0 / soft_total)[:, None]
    logit_gradient = ((likelihood - codes.astype(jnp.float32)) / sharpness_divisor).astype(
        jnp.bfloat16
    )

    proto_part = contract_rows(logit_gradient, views)
    view_part = jnp.dot(logit_gradient, protos, preferred_element_type=jnp.float32)

    y, z, x, core = (lax.axis_index(name) for name in ("y", "z", "x", "core"))
    y_count, z_count, x_count = (lax.axis_size(name) for name in ("y", "z", "x"))

    def mine(value, outer, outer_count, inner, inner_count):
        return block(block(value, outer, outer_count), inner, inner_count)

    view_sum = scatter_sum(scatter_sum(view_part, "core"), "x")
    proto_sum = scatter_sum(proto_part, "y")
    proto_sum = lax.all_to_all(
        proto_sum.reshape(z_count, -1, proto_sum.shape[1]), "z", 0, 0, tiled=True
    ).sum(axis=0)
    emb_rows = unit_rows(mine(embeddings, core, 2, x, x_count))
    proto_rows = unit_rows(mine(prototypes, y, y_count, z, z_count))
    emb_piece = norm_back(view_sum, *emb_rows)
    proto_piece = norm_back(proto_sum, *proto_rows)
    emb_grad = gather_blocks(gather_blocks(emb_piece, "x"), "core")
    proto_grad = gathered(proto_piece, "z").reshape(-1, proto_piece.shape[1])
    proto_grad = gather_blocks(proto_grad, "y")
    return (emb_grad, proto_grad)


def solution(mesh):
    inner = Mesh(mesh.devices.reshape(16, 4, 4, 2), ("z", "y", "x", "core"))
    return jax.shard_map(
        body,
        mesh=inner,
        in_specs=(P(rows_axes, None), P(proto_axes, None), P(rows_axes)),
        out_specs=(P(rows_axes, None), P(proto_axes, None)),
        check_vma=False,
    )
```

```python
import functools

import jax
import jax.numpy as jnp
from jax import lax
from jax.experimental import pallas as pl
from jax.experimental.pallas import tpu as pltpu
from jax.sharding import Mesh, PartitionSpec as P

ITERS = 3


epsilon_code = 0.05
sharpness_divisor = 0.1
norm_floor = 1e-06
rows_axes = ("z", "y")
proto_axes = ("x", "core")
LANES = 128
ROWS = 256
f32 = jnp.float32
bf16 = jnp.bfloat16


def shifted(value, axis, steps):
    count = lax.axis_size(axis)
    pairs = [(source, (source + steps) % count) for source in range(count)]
    return lax.ppermute(value, axis, pairs)


def exchanged(value, axis):
    return lax.all_to_all(value, axis, 0, 0, tiled=True)


def gathered(value, axis):
    return exchanged(jnp.broadcast_to(value[None], (lax.axis_size(axis),) + value.shape), axis)


def unit_rows(values):
    wide = values.astype(f32)
    scale = lax.rsqrt(jnp.mean(wide * wide, axis=1, keepdims=True) + norm_floor) / jnp.sqrt(
        f32(wide.shape[1])
    )
    return (wide * scale, scale)


def norm_back(upstream, units, scale):
    return scale * (upstream - units * jnp.sum(units * upstream, axis=1, keepdims=True))


def block(value, index, count):
    size = value.shape[0] // count
    return lax.dynamic_slice_in_dim(value, index * size, size, 0)


def kernel_units(values):
    wide = values.astype(f32)
    mean = jnp.sum(wide * wide, axis=1, keepdims=True) * (1.0 / wide.shape[1])
    scale = lax.rsqrt(mean + norm_floor) * (1.0 / wide.shape[1] ** 0.5)
    return (wide * scale).astype(bf16)


def lane_sums(values):
    total = values[:, :LANES]
    for start in range(LANES, values.shape[1], LANES):
        total = total + values[:, start : start + LANES]
    return total


def as_row(partials):
    return jnp.sum(partials.T, axis=0, keepdims=True)


def as_column(row):
    return jnp.broadcast_to(row, (LANES, row.shape[1])).T


def tempered_kernel(emb_ref, proto_ref, temp_ref, views_ref, protos_ref, col_ref, soft_ref):
    protos_ref[...] = kernel_units(proto_ref[...])
    views_ref[...] = kernel_units(emb_ref[...])
    col_ref[...] = jnp.zeros_like(col_ref)

    @pl.loop(0, emb_ref.shape[0] // ROWS)
    def _(step):
        rows = pl.ds(pl.multiple_of(step * ROWS, ROWS), ROWS)
        scores = lax.dot_general(
            views_ref[rows, :],
            protos_ref[...],
            (((1,), (1,)), ((), ())),
            preferred_element_type=f32,
        )
        tempered = jnp.exp(scores * (1.0 / sharpness_divisor))
        temp_ref[rows, :] = tempered
        col_ref[...] += jnp.sum(tempered * tempered, axis=0, keepdims=True)
        soft_ref[:, rows] = as_row(lane_sums(tempered))


def codes_kernel(emb_ref, protos_ref, kernel_ref):
    @pl.loop(0, emb_ref.shape[0] // ROWS)
    def _(step):
        rows = pl.ds(pl.multiple_of(step * ROWS, ROWS), ROWS)
        scores = lax.dot_general(
            kernel_units(emb_ref[rows, :]),
            protos_ref[...],
            (((1,), (1,)), ((), ())),
            preferred_element_type=f32,
        )
        kernel_ref[rows, :] = jnp.exp(scores * (1.0 / epsilon_code))


def row_kernel(squared, temp_ref, totals_ref, row_ref):
    column_scale = 1.0 / jnp.sum(totals_ref[:, 0, :], axis=0, keepdims=True)

    @pl.loop(0, temp_ref.shape[0] // ROWS)
    def _(step):
        rows = pl.ds(pl.multiple_of(step * ROWS, ROWS), ROWS)
        value = temp_ref[rows, :]
        value = value * value if squared else value
        row_ref[:, rows] = as_row(lane_sums(value * column_scale))


def col_kernel(temp_ref, totals_ref, col_ref):
    count = temp_ref.shape[0]
    weight = 1.0 / jnp.sum(totals_ref[:, 0, :count], axis=0, keepdims=True)
    col_ref[...] = jnp.zeros_like(col_ref)
    for step in range(count // ROWS):
        wide = as_column(weight[:, step * ROWS : (step + 1) * ROWS])
        for start in range(0, temp_ref.shape[1], LANES):
            value = temp_ref[step * ROWS : (step + 1) * ROWS, start : start + LANES]
            col_ref[:, start : start + LANES] += jnp.sum(value * value * wide, axis=0, keepdims=True)


def gradient_kernel(
    temp_ref, other_ref, totals_ref, line_ref, soft_ref, views_ref, protos_ref, view_ref, proto_ref
):
    count = temp_ref.shape[0]
    column_scale = 1.0 / jnp.sum(totals_ref[:, 0, :], axis=0, keepdims=True)
    line = 1.0 / jnp.sum(line_ref[:, 0, :], axis=0, keepdims=True)
    soft = 1.0 / jnp.sum(soft_ref[:, 0, count:], axis=0, keepdims=True)
    proto_ref[...] = jnp.zeros_like(proto_ref)
    for step in range(count // ROWS):
        rows = slice(step * ROWS, (step + 1) * ROWS)
        line_wide = as_column(line[:, rows])[:, :1]
        soft_wide = as_column(soft[:, rows])[:, :1]
        codes = (other_ref[rows, :] * column_scale * line_wide).astype(bf16)
        likelihood = temp_ref[rows, :] * soft_wide
        grad = ((likelihood - codes.astype(f32)) * (1.0 / sharpness_divisor)).astype(bf16)
        view_ref[rows, :] = jnp.dot(grad, protos_ref[...], preferred_element_type=f32)
        proto_ref[...] += lax.dot_general(
            grad, views_ref[rows, :], (((0,), (0,)), ((), ())), preferred_element_type=f32
        )


def call(kernel, name, out_shape, *args, flops, size, exps=0, limit=16):
    return pl.pallas_call(
        kernel,
        name=name,
        out_shape=out_shape,
        in_specs=[pl.BlockSpec(memory_space=pltpu.VMEM)] * len(args),
        out_specs=jax.tree.map(lambda _: pl.BlockSpec(memory_space=pltpu.VMEM), out_shape),
        compiler_params=pltpu.CompilerParams(vmem_limit_bytes=limit * 2**20),
        cost_estimate=pl.CostEstimate(flops=flops, bytes_accessed=size, transcendentals=exps),
    )(*args)


def body(embeddings, prototypes, partner):
    count, width = embeddings.shape
    slots = prototypes.shape[0]
    shape = jax.ShapeDtypeStruct
    entries = count * slots
    links = jnp.remainder(partner, count)
    sent = shifted(embeddings, "z", lax.axis_size("z") // 2)

    tempered, views, protos, column_part, soft_part = call(
        tempered_kernel,
        "tempered",
        (
            pltpu.VMEM((count, slots), f32),
            shape((count, width), bf16),
            shape((slots, width), bf16),
            shape((1, slots), f32),
            shape((1, count), f32),
        ),
        embeddings,
        prototypes,
        flops=2 * entries * width,
        size=4 * entries,
        exps=entries,
    )

    def column_totals(part):
        return gathered(lax.psum(part, "y"), "z")

    def row_pass(squared, values, totals):
        return call(
            functools.partial(row_kernel, squared),
            "row_pass",
            shape((1, count), f32),
            values,
            totals,
            flops=3 * entries,
            size=4 * entries,
        )

    def column_pass(values, totals):
        return call(
            col_kernel,
            "column_pass",
            shape((1, slots), f32),
            values,
            totals,
            flops=3 * entries,
            size=4 * entries,
        )

    column_total = column_totals(column_part)
    row_part = row_pass(True, tempered, column_total)
    first = gathered(jnp.concatenate([row_part, soft_part], axis=1), proto_axes)
    first, sent = lax.optimization_barrier((first, sent))
    other = sent[links]
    column_total = column_totals(column_pass(tempered, first))
    for sweep in range(ITERS - 2):
        row_total = gathered(row_pass(True, tempered, column_total), proto_axes)
        column_total = column_totals(column_pass(tempered, row_total))
    other_kernel = call(
        codes_kernel,
        "partner_codes",
        pltpu.VMEM((count, slots), f32),
        other,
        protos,
        flops=2 * entries * width,
        size=4 * entries,
        exps=entries,
    )
    line_total = gathered(row_pass(False, other_kernel, column_total), proto_axes)
    view_part, proto_part = call(
        gradient_kernel,
        "gradient",
        (shape((count, width), f32), shape((slots, width), f32)),
        tempered,
        other_kernel,
        column_total,
        line_total,
        first,
        views,
        protos,
        flops=4 * entries * width,
        size=8 * entries,
    )

    y, z, x, core = (lax.axis_index(name) for name in ("y", "z", "x", "core"))
    y_count, z_count, x_count = (lax.axis_size(name) for name in ("y", "z", "x"))

    view_sum = exchanged(view_part.reshape(2 * x_count, -1, width), proto_axes).sum(axis=0)
    proto_sum = exchanged(proto_part.reshape(y_count, -1, width), "y").sum(axis=0)
    proto_sum = exchanged(proto_sum.reshape(z_count, -1, width), "z").sum(axis=0)
    emb_rows = unit_rows(block(embeddings, x * 2 + core, 2 * x_count))
    proto_rows = unit_rows(block(prototypes, y * z_count + z, y_count * z_count))
    emb_grad = gathered(norm_back(view_sum, *emb_rows), proto_axes).reshape(count, width)
    proto_grad = gathered(norm_back(proto_sum, *proto_rows), "z").reshape(-1, width)
    proto_grad = gathered(proto_grad, "y").reshape(slots, width)
    return (emb_grad, proto_grad)


def solution(mesh):
    inner = Mesh(mesh.devices.reshape(16, 4, 4, 2), ("z", "y", "x", "core"))
    return jax.shard_map(
        body,
        mesh=inner,
        in_specs=(P(rows_axes, None), P(proto_axes, None), P(rows_axes)),
        out_specs=(P(rows_axes, None), P(proto_axes, None)),
        check_vma=False,
    )
```

```python
import functools

import jax
import jax.numpy as jnp
from jax import lax
from jax.experimental import pallas as pl
from jax.experimental.pallas import tpu as pltpu
from jax.sharding import Mesh, PartitionSpec as P

ITERS = 3


epsilon_code = 0.05
sharpness_divisor = 0.1
norm_floor = 1e-06
rows_axes = ("z", "y")
proto_axes = ("x", "core")
LANES = 128
ROWS = 128
f32 = jnp.float32
bf16 = jnp.bfloat16
SENT = jnp.float16
FOLD = 8


def shifted(value, axis, steps):
    count = lax.axis_size(axis)
    pairs = [(source, (source + steps) % count) for source in range(count)]
    return lax.ppermute(value, axis, pairs)


def exchanged(value, axis):
    return lax.all_to_all(value, axis, 0, 0, tiled=True)


def gathered(value, axis):
    return exchanged(jnp.broadcast_to(value[None], (lax.axis_size(axis),) + value.shape), axis)


def unit_rows(values):
    wide = values.astype(f32)
    scale = lax.rsqrt(jnp.mean(wide * wide, axis=1, keepdims=True) + norm_floor) / jnp.sqrt(
        f32(wide.shape[1])
    )
    return (wide * scale, scale)


def row_scale(values):
    return unit_rows(values)[1]


def tangent(upstream, units):
    return upstream - units * jnp.sum(units * upstream, axis=1, keepdims=True)


def total(pieces):
    return jnp.sum(pieces.astype(f32), axis=0)


def block(value, index, count):
    size = value.shape[0] // count
    return lax.dynamic_slice_in_dim(value, index * size, size, 0)


def scatter_sum(value, axis):
    count = lax.axis_size(axis)
    me = lax.axis_index(axis)
    total = block(value, me, count).astype(f32)
    for step in range(1, count):
        piece = shifted(block(value, (me + step) % count, count), axis, step)
        total = total + piece.astype(f32)
    return total.astype(value.dtype)


def gather_blocks(value, axis):
    count = lax.axis_size(axis)
    me = lax.axis_index(axis)
    pieces = [value] + [shifted(value, axis, step) for step in range(1, count)]
    out = jnp.zeros((count,) + value.shape, value.dtype)
    for step, piece in enumerate(pieces):
        out = lax.dynamic_update_slice_in_dim(out, piece[None], (me + count - step) % count, 0)
    return out.reshape((-1,) + value.shape[1:])


def kernel_units(values):
    wide = values.astype(f32)
    mean = jnp.sum(wide * wide, axis=1, keepdims=True) * (1.0 / wide.shape[1])
    scale = lax.rsqrt(mean + norm_floor) * (1.0 / wide.shape[1] ** 0.5)
    return (wide * scale).astype(bf16)


def lane_sums(values):
    total = values[:, :LANES]
    for start in range(LANES, values.shape[1], LANES):
        total = total + values[:, start : start + LANES]
    return total


def as_row(partials):
    return jnp.sum(partials.T, axis=0, keepdims=True)


def as_column(row):
    return jnp.broadcast_to(row, (LANES, row.shape[1])).T


def column_tile(values, start):
    width = values.shape[1]
    return values[start // width : start // width + 1, start % width : start % width + LANES]


def add_column(ref, start, values):
    width = ref.shape[1]
    at = (slice(start // width, start // width + 1), slice(start % width, start % width + LANES))
    ref[at] += jnp.sum(values, axis=0, keepdims=True)


def tempered_kernel(emb_ref, proto_ref, temp_ref, views_ref, protos_ref, col_ref, soft_ref):
    @pl.when(pl.program_id(0) == 0)
    def _():
        protos_ref[...] = kernel_units(proto_ref[...])
        col_ref[...] = jnp.zeros_like(col_ref)

    views = kernel_units(emb_ref[...])
    views_ref[...] = views
    scores = lax.dot_general(
        views, protos_ref[...], (((1,), (1,)), ((), ())), preferred_element_type=f32
    )
    tempered = jnp.exp(scores * (1.0 / sharpness_divisor))
    temp_ref[...] = tempered
    for start in range(0, tempered.shape[1], LANES):
        value = tempered[:, start : start + LANES]
        add_column(col_ref, start, value * value)
    soft_ref[...] = as_row(lane_sums(tempered))


def codes_kernel(emb_ref, protos_ref, kernel_ref):
    scores = lax.dot_general(
        kernel_units(emb_ref[...]),
        protos_ref[...],
        (((1,), (1,)), ((), ())),
        preferred_element_type=f32,
    )
    kernel_ref[...] = jnp.exp(scores * (1.0 / epsilon_code))


def row_kernel(squared, temp_ref, totals_ref, *refs):
    row_ref = refs[-1]
    column_scale = 1.0 / jnp.sum(totals_ref[...], axis=0)
    total = jnp.zeros((temp_ref.shape[0], LANES), f32)
    for start in range(0, temp_ref.shape[1], LANES):
        value = temp_ref[:, start : start + LANES]
        value = value * value if squared else value
        total = total + value * column_tile(column_scale, start)
    rows = as_row(total)
    for to in range(row_ref.shape[0]):
        row_ref[to, :1, :] = rows
        if len(refs) > 1:
            row_ref[to, 1:, :] = refs[0][...]


def col_kernel(temp_ref, totals_ref, col_ref):
    @pl.when(pl.program_id(0) == 0)
    def _():
        col_ref[...] = jnp.zeros_like(col_ref)

    wide = as_column(1.0 / jnp.sum(totals_ref[:, 0, :], axis=0, keepdims=True))
    for start in range(0, temp_ref.shape[1], LANES):
        value = temp_ref[:, start : start + LANES]
        add_column(col_ref, start, value * value * wide)


def gradient_kernel(
    temp_ref, other_ref, totals_ref, line_ref, soft_ref, views_ref, protos_ref, view_ref, proto_ref, sum_ref
):
    step = pl.program_id(0)

    @pl.when(step == 0)
    def _():
        sum_ref[...] = jnp.zeros_like(sum_ref)

    column_scale = 1.0 / jnp.sum(totals_ref[...], axis=0)
    line = as_column(1.0 / jnp.sum(line_ref[:, 0, :], axis=0, keepdims=True))
    soft = as_column(1.0 / jnp.sum(soft_ref[:, 1, :], axis=0, keepdims=True))
    grads = []
    for start in range(0, temp_ref.shape[1], LANES):
        tile = slice(start, start + LANES)
        codes = (other_ref[:, tile] * column_tile(column_scale, start) * line).astype(bf16)
        likelihood = temp_ref[:, tile] * soft
        grads.append(
            ((likelihood - codes.astype(f32)) * (1.0 / sharpness_divisor)).astype(bf16)
        )
    grad = jnp.concatenate(grads, axis=1)
    view = jnp.dot(grad, protos_ref[...], preferred_element_type=f32)
    view_ref[...] = view.astype(view_ref.dtype)
    sum_ref[...] += lax.dot_general(
        grad, views_ref[...], (((0,), (0,)), ((), ())), preferred_element_type=f32
    )

    @pl.when(step == pl.num_programs(0) - 1)
    def _():
        proto_ref[...] = sum_ref[...].astype(proto_ref.dtype)


def whole(shape):
    return pl.BlockSpec(shape, lambda i: (0,) * len(shape))


def strip(shape, rows):
    return pl.BlockSpec((rows, shape[1]), lambda i: (i, 0))


def span(shape, rows):
    last = len(shape) - 1
    return pl.BlockSpec(shape[:-1] + (rows,), lambda i: (0,) * last + (i,))


def in_hbm(value):
    return pltpu.with_memory_space_constraint(value, pltpu.HBM)


def call(kernel, name, ins, outs, flops, size, exps=0, rows=ROWS, scratch=()):
    return pl.pallas_call(
        kernel,
        name=name,
        grid=(ins[0][0].shape[0] // rows,),
        out_shape=[jax.ShapeDtypeStruct(shape, kind) for shape, kind, _ in outs],
        in_specs=[spec for _, spec in ins],
        out_specs=[spec for _, _, spec in outs],
        scratch_shapes=scratch,
        compiler_params=pltpu.CompilerParams(vmem_limit_bytes=16 * 2**20),
        cost_estimate=pl.CostEstimate(flops=flops, bytes_accessed=size, transcendentals=exps),
    )(*[value for value, _ in ins])


def body(embeddings, prototypes, partner):
    count, width = embeddings.shape
    slots = prototypes.shape[0]
    entries = count * slots
    links = jnp.remainder(partner, count)
    y, z, x, core = (lax.axis_index(name) for name in ("y", "z", "x", "core"))
    y_count, z_count, x_count = (lax.axis_size(name) for name in ("y", "z", "x"))
    own = block(embeddings, x * 2 + core, 2 * x_count)
    sent = gathered(shifted(own, "z", z_count // 2), proto_axes).reshape(count, width)

    matrix, row, column = (count, slots), (1, count), (FOLD, slots // FOLD)
    members = 2 * x_count
    tempered, views, protos, column_part, soft_part = call(
        tempered_kernel,
        "tempered",
        [(embeddings, strip(embeddings.shape, ROWS)), (prototypes, whole(prototypes.shape))],
        [
            (matrix, f32, strip(matrix, ROWS)),
            ((count, width), bf16, strip((count, width), ROWS)),
            ((slots, width), bf16, whole((slots, width))),
            (column, f32, whole(column)),
            (row, f32, span(row, ROWS)),
        ],
        flops=2 * entries * width,
        size=4 * entries,
        exps=entries,
    )
    tempered = in_hbm(tempered)

    def column_totals(part):
        return gathered(lax.psum(part, "y"), "z")

    def row_totals(squared, values, totals, *soft):
        sums = (members, 1 + len(soft), count)
        (part,) = call(
            functools.partial(row_kernel, squared),
            "row_pass",
            [(values, strip(matrix, ROWS)), (totals, whole(totals.shape))]
            + [(value, span(row, ROWS)) for value in soft],
            [(sums, f32, span(sums, ROWS))],
            flops=3 * entries,
            size=4 * entries,
        )
        return exchanged(part, proto_axes)

    def column_pass(values, totals):
        return call(
            col_kernel,
            "column_pass",
            [(values, strip(matrix, ROWS)), (totals, span(totals.shape, ROWS))],
            [(column, f32, whole(column))],
            flops=3 * entries,
            size=4 * entries,
        )[0]

    column_total = column_totals(column_part)
    first = row_totals(True, tempered, column_total, soft_part)
    first, sent = lax.optimization_barrier((first, sent))
    other = sent[links]
    column_total = column_totals(column_pass(tempered, first))
    for sweep in range(ITERS - 2):
        row_total = row_totals(True, tempered, column_total)
        column_total = column_totals(column_pass(tempered, row_total))
    (other_kernel,) = call(
        codes_kernel,
        "partner_codes",
        [(other, strip(other.shape, ROWS)), (protos, whole(protos.shape))],
        [(matrix, f32, strip(matrix, ROWS))],
        flops=2 * entries * width,
        size=4 * entries,
        exps=entries,
    )
    other_kernel = in_hbm(other_kernel)
    line_total = row_totals(False, other_kernel, column_total)
    view_part, proto_part = call(
        gradient_kernel,
        "gradient",
        [
            (tempered, strip(matrix, ROWS)),
            (other_kernel, strip(matrix, ROWS)),
            (column_total, whole(column_total.shape)),
            (line_total, span(line_total.shape, ROWS)),
            (first, span(first.shape, ROWS)),
            (views, strip(views.shape, ROWS)),
            (protos, whole(protos.shape)),
        ],
        [
            ((count, width), f32, strip((count, width), ROWS)),
            ((slots, width), f32, whole((slots, width))),
        ],
        flops=4 * entries * width,
        size=8 * entries,
        scratch=[pltpu.VMEM((slots, width), f32)],
    )

    proto_rows = unit_rows(block(prototypes, y * z_count + z, y_count * z_count))[0]
    view_rows = unit_rows(block(embeddings, core * x_count + x, members))[0]
    proto_pieces = exchanged(proto_part.astype(SENT).reshape(y_count, -1, width), "y")
    proto_sum = total(proto_pieces).astype(SENT)
    proto_pieces = exchanged(proto_sum.reshape(z_count, -1, width), "z")
    proto_sum = (tangent(total(proto_pieces), proto_rows) * (1.0 / z_count)).astype(SENT)
    proto_sum = gathered(proto_sum, "z").reshape(-1, width)

    view_sum = scatter_sum(scatter_sum(view_part.astype(SENT), "core"), "x")
    view_sum = tangent(view_sum.astype(f32), view_rows).astype(SENT)
    view_sum = gather_blocks(gather_blocks(view_sum, "x"), "core")

    proto_sum = gathered(proto_sum, "y").reshape(slots, width)
    emb_grad = row_scale(embeddings) * view_sum.astype(f32)
    proto_grad = row_scale(prototypes) * float(z_count) * proto_sum.astype(f32)
    return (emb_grad, proto_grad)


def solution(mesh):
    inner = Mesh(mesh.devices.reshape(16, 4, 4, 2), ("z", "y", "x", "core"))
    return jax.shard_map(
        body,
        mesh=inner,
        in_specs=(P(rows_axes, None), P(proto_axes, None), P(rows_axes)),
        out_specs=(P(rows_axes, None), P(proto_axes, None)),
        check_vma=False,
    )
```

```python
import functools

import jax
import jax.numpy as jnp
from jax import lax
from jax.experimental import pallas as pl
from jax.experimental.pallas import tpu as pltpu
from jax.sharding import Mesh, PartitionSpec as P

ITERS = 3


epsilon_code = 0.05
sharpness_divisor = 0.1
norm_floor = 1e-06
rows_axes = ("z", "y")
proto_axes = ("x", "core")
LANES = 128
ROWS = 256
f32 = jnp.float32
bf16 = jnp.bfloat16
SENT = jnp.float16
FOLD = 8


def shifted(value, axis, steps):
    count = lax.axis_size(axis)
    pairs = [(source, (source + steps) % count) for source in range(count)]
    return lax.ppermute(value, axis, pairs)


def exchanged(value, axis):
    return lax.all_to_all(value, axis, 0, 0, tiled=True)


def gathered(value, axis):
    return exchanged(jnp.broadcast_to(value[None], (lax.axis_size(axis),) + value.shape), axis)


def unit_rows(values):
    wide = values.astype(f32)
    scale = lax.rsqrt(jnp.mean(wide * wide, axis=1, keepdims=True) + norm_floor) / jnp.sqrt(
        f32(wide.shape[1])
    )
    return (wide * scale, scale)


def row_scale(values):
    return unit_rows(values)[1]


def tangent(upstream, units):
    return upstream - units * jnp.sum(units * upstream, axis=1, keepdims=True)


def total(pieces):
    return jnp.sum(pieces.astype(f32), axis=0)


def block(value, index, count):
    size = value.shape[0] // count
    return lax.dynamic_slice_in_dim(value, index * size, size, 0)


def scatter_sum(value, axis):
    count = lax.axis_size(axis)
    me = lax.axis_index(axis)
    total = block(value, me, count).astype(f32)
    for step in range(1, count):
        piece = shifted(block(value, (me + step) % count, count), axis, step)
        total = total + piece.astype(f32)
    return total.astype(value.dtype)


def gather_blocks(value, axis):
    count = lax.axis_size(axis)
    me = lax.axis_index(axis)
    pieces = [value] + [shifted(value, axis, step) for step in range(1, count)]
    out = jnp.zeros((count,) + value.shape, value.dtype)
    for step, piece in enumerate(pieces):
        out = lax.dynamic_update_slice_in_dim(out, piece[None], (me + count - step) % count, 0)
    return out.reshape((-1,) + value.shape[1:])


def kernel_units(values):
    wide = values.astype(f32)
    mean = jnp.sum(wide * wide, axis=1, keepdims=True) * (1.0 / wide.shape[1])
    scale = lax.rsqrt(mean + norm_floor) * (1.0 / wide.shape[1] ** 0.5)
    return (wide * scale).astype(bf16)


def as_row(partials):
    return jnp.sum(partials.T, axis=0, keepdims=True)


def as_column(row):
    return jnp.broadcast_to(row, (LANES, row.shape[1])).T


def column_tile(values, start):
    width = values.shape[1]
    return values[start // width : start // width + 1, start % width : start % width + LANES]


def add_column(ref, start, values):
    width = ref.shape[2]
    tile = (0, slice(start // width, start // width + 1), slice(start % width, start % width + LANES))
    ref[tile] += jnp.sum(values, axis=0, keepdims=True)


def tiles(matrix):
    return range(0, matrix.shape[1], LANES)


def tempered_rows(units, protos_ref, divisor):
    scores = lax.dot_general(
        units, protos_ref[...], (((1,), (1,)), ((), ())), preferred_element_type=f32
    )
    return jnp.exp(scores * (1.0 / divisor))


def steps(count):
    return [slice(start, start + ROWS) for start in range(0, count, ROWS)]


def for_each_receiver(ref):
    for to in range(1, ref.shape[0]):
        ref[to] = ref[0]


def first_kernel(emb_ref, proto_ref, views_ref, protos_ref, col_ref):
    protos_ref[...] = kernel_units(proto_ref[...])
    views_ref[...] = kernel_units(emb_ref[...])
    col_ref[0] = jnp.zeros_like(col_ref[0])

    @pl.loop(0, emb_ref.shape[0] // ROWS)
    def _(step):
        rows = pl.ds(pl.multiple_of(step * ROWS, ROWS), ROWS)
        tempered = tempered_rows(views_ref[rows, :], protos_ref, sharpness_divisor)
        for start in tiles(tempered):
            value = tempered[:, start : start + LANES]
            add_column(col_ref, start, value * value)

    for_each_receiver(col_ref)


def rows_kernel(own, emb_ref, protos_ref, totals_ref, temp_ref, row_ref):
    column_scale = 1.0 / jnp.sum(totals_ref[...], axis=0)

    @pl.loop(0, emb_ref.shape[0] // ROWS)
    def _(step):
        rows = pl.ds(pl.multiple_of(step * ROWS, ROWS), ROWS)
        units = emb_ref[rows, :]
        if own:
            tempered = tempered_rows(units, protos_ref, sharpness_divisor)
        else:
            tempered = tempered_rows(kernel_units(units), protos_ref, epsilon_code)
        temp_ref[rows, :] = tempered
        total = soft = jnp.zeros((ROWS, LANES), f32)
        for start in tiles(tempered):
            value = tempered[:, start : start + LANES]
            if own:
                soft = soft + value
                value = value * value
            total = total + value * column_tile(column_scale, start)
        row_ref[0, :1, rows] = as_row(total)
        if own:
            row_ref[0, 1:, rows] = as_row(soft)

    for_each_receiver(row_ref)


def row_kernel(temp_ref, totals_ref, row_ref):
    column_scale = 1.0 / jnp.sum(totals_ref[...], axis=0)
    for rows in steps(temp_ref.shape[0]):
        total = jnp.zeros((ROWS, LANES), f32)
        for start in tiles(temp_ref):
            value = temp_ref[rows, start : start + LANES]
            total = total + value * value * column_tile(column_scale, start)
        row_ref[0, :, rows] = as_row(total)
    for_each_receiver(row_ref)


def col_kernel(temp_ref, totals_ref, col_ref):
    weight = 1.0 / jnp.sum(totals_ref[:, 0, :], axis=0, keepdims=True)
    col_ref[0] = jnp.zeros_like(col_ref[0])
    for rows in steps(temp_ref.shape[0]):
        wide = as_column(weight[:, rows])
        for start in tiles(temp_ref):
            value = temp_ref[rows, start : start + LANES]
            add_column(col_ref, start, value * value * wide)
    for_each_receiver(col_ref)


def gradient_kernel(
    other_ref, totals_ref, line_ref, soft_ref, views_ref, protos_ref, view_ref, proto_ref
):
    proto_ref[...] = jnp.zeros_like(proto_ref)
    column_scale = 1.0 / jnp.sum(totals_ref[...], axis=0)
    line_row = 1.0 / jnp.sum(line_ref[:, 0, :], axis=0, keepdims=True)
    soft_row = 1.0 / jnp.sum(soft_ref[:, 1, :], axis=0, keepdims=True)
    for rows in steps(other_ref.shape[0]):
        line = as_column(line_row[:, rows])
        soft = as_column(soft_row[:, rows])
        views = views_ref[rows, :]
        tempered = tempered_rows(views, protos_ref, sharpness_divisor)
        grads = []
        for start in tiles(tempered):
            codes = other_ref[rows, start : start + LANES]
            codes = (codes * column_tile(column_scale, start) * line).astype(bf16)
            likelihood = tempered[:, start : start + LANES] * soft
            grads.append(
                ((likelihood - codes.astype(f32)) * (1.0 / sharpness_divisor)).astype(bf16)
            )
        grad = jnp.concatenate(grads, axis=1)
        view_ref[rows, :] = jnp.dot(grad, protos_ref[...], preferred_element_type=f32)
        proto_ref[...] += lax.dot_general(
            grad, views, (((0,), (0,)), ((), ())), preferred_element_type=f32
        )


def call(kernel, name, ins, outs, flops, size, exps=0):
    in_vmem = pl.BlockSpec(memory_space=pltpu.VMEM)
    return pl.pallas_call(
        kernel,
        name=name,
        out_shape=[jax.ShapeDtypeStruct(shape, kind) for shape, kind in outs],
        in_specs=[in_vmem] * len(ins),
        out_specs=[in_vmem] * len(outs),
        compiler_params=pltpu.CompilerParams(vmem_limit_bytes=16 * 2**20),
        cost_estimate=pl.CostEstimate(flops=flops, bytes_accessed=size, transcendentals=exps),
    )(*ins)


def body(embeddings, prototypes, partner):
    count, width = embeddings.shape
    slots = prototypes.shape[0]
    entries = count * slots
    links = jnp.remainder(partner, count)
    y, z, x, core = (lax.axis_index(name) for name in ("y", "z", "x", "core"))
    y_count, z_count, x_count = (lax.axis_size(name) for name in ("y", "z", "x"))
    matrix, column = (count, slots), (FOLD, slots // FOLD)
    members = 2 * x_count
    own = block(embeddings, x * 2 + core, members)
    sent = shifted(own, "z", z_count // 2)
    views, protos, column_part = call(
        first_kernel,
        "first",
        [embeddings, prototypes],
        [((count, width), bf16), ((slots, width), bf16), ((y_count,) + column, f32)],
        flops=2 * entries * width,
        size=4 * slots * width,
        exps=entries,
    )

    def tempered_pass(mine, rows, totals):
        tempered, part = call(
            functools.partial(rows_kernel, mine),
            "tempered_pass",
            [rows, protos, totals],
            [(matrix, f32), ((members, 2 if mine else 1, count), f32)],
            flops=2 * entries * width,
            size=4 * slots * width,
            exps=entries,
        )
        return tempered, exchanged(part, proto_axes)

    def row_pass(tempered, totals):
        sums = ((members, 1, count), f32)
        (part,) = call(row_kernel, "row_pass", [tempered, totals], [sums], 3 * entries, 4 * count)
        return exchanged(part, proto_axes)

    def column_pass(tempered, totals):
        sums = ((y_count,) + column, f32)
        (part,) = call(col_kernel, "column_pass", [tempered, totals], [sums], 3 * entries, 4 * count)
        return total(exchanged(part, "y"))

    column_part, sent = lax.optimization_barrier((total(exchanged(column_part, "y")), sent))
    sent = gather_blocks(gather_blocks(sent, "core"), "x")
    column_total, sent = lax.optimization_barrier((gathered(column_part, "z"), sent))
    tempered, first = tempered_pass(True, views, column_total)
    for sweep in range(1, ITERS):
        row_total = row_pass(tempered, column_total) if sweep > 1 else first
        column_part = column_pass(tempered, row_total)
        if sweep == ITERS - 1:
            column_part, sent = lax.optimization_barrier((column_part, sent))
        column_total = gathered(column_part, "z")
    other_kernel, line_total = tempered_pass(False, sent[links], column_total)
    view_part, proto_part = call(
        gradient_kernel,
        "gradient",
        [other_kernel, column_total, line_total, first, views, protos],
        [((count, width), f32), ((slots, width), f32)],
        flops=6 * entries * width,
        size=8 * slots * width,
        exps=entries,
    )

    proto_rows = unit_rows(block(prototypes, y * z_count + z, y_count * z_count))[0]
    view_rows = unit_rows(block(embeddings, core * x_count + x, members))[0]
    proto_pieces = exchanged(proto_part.astype(SENT).reshape(y_count, -1, width), "y")
    proto_sum = total(proto_pieces).astype(SENT)
    proto_pieces = exchanged(proto_sum.reshape(z_count, -1, width), "z")
    proto_sum = (tangent(total(proto_pieces), proto_rows) * (1.0 / z_count)).astype(SENT)
    proto_sum = gathered(proto_sum, "z").reshape(-1, width)

    view_sum = scatter_sum(scatter_sum(view_part.astype(SENT), "core"), "x")
    view_sum = tangent(view_sum.astype(f32), view_rows).astype(SENT)
    view_sum = gather_blocks(gather_blocks(view_sum, "x"), "core")

    proto_sum = gathered(proto_sum, "y").reshape(slots, width)
    emb_grad = row_scale(embeddings) * view_sum.astype(f32)
    proto_grad = row_scale(prototypes) * float(z_count) * proto_sum.astype(f32)
    return (emb_grad, proto_grad)


def solution(mesh):
    inner = Mesh(mesh.devices.reshape(16, 4, 4, 2), ("z", "y", "x", "core"))
    return jax.shard_map(
        body,
        mesh=inner,
        in_specs=(P(rows_axes, None), P(proto_axes, None), P(rows_axes)),
        out_specs=(P(rows_axes, None), P(proto_axes, None)),
        check_vma=False,
    )
```

```python
import functools

import jax
import jax.numpy as jnp
from jax import lax
from jax.experimental import pallas as pl
from jax.experimental.pallas import tpu as pltpu
from jax.sharding import Mesh, PartitionSpec as P

ITERS = 3


epsilon_code = 0.05
sharpness_divisor = 0.1
norm_floor = 1e-06
rows_axes = ("z", "y")
proto_axes = ("x", "core")
LANES = 128
ROWS = 256
f32 = jnp.float32
bf16 = jnp.bfloat16
SENT = jnp.float16
FOLD = 8
LOG2_E = 1.4426950408889634


def shifted(value, axis, steps):
    count = lax.axis_size(axis)
    pairs = [(source, (source + steps) % count) for source in range(count)]
    return lax.ppermute(value, axis, pairs)


def exchanged(value, axis):
    return lax.all_to_all(value, axis, 0, 0, tiled=True)


def gathered(value, axis):
    return exchanged(jnp.broadcast_to(value[None], (lax.axis_size(axis),) + value.shape), axis)


def unit_rows(values):
    wide = values.astype(f32)
    scale = lax.rsqrt(jnp.mean(wide * wide, axis=1, keepdims=True) + norm_floor) / jnp.sqrt(
        f32(wide.shape[1])
    )
    return (wide * scale, scale)


def row_scale(values):
    return unit_rows(values)[1]


def tangent(upstream, units):
    return upstream - units * jnp.sum(units * upstream, axis=1, keepdims=True)


def total(pieces):
    parts = [pieces[index].astype(f32) for index in range(pieces.shape[0])]
    while len(parts) > 1:
        parts = [left + right for left, right in zip(parts[::2], parts[1::2], strict=True)]
    return parts[0]


def block(value, index, count):
    size = value.shape[0] // count
    return lax.dynamic_slice_in_dim(value, index * size, size, 0)


def scatter_sum(value, axis):
    count = lax.axis_size(axis)
    me = lax.axis_index(axis)
    total = block(value, me, count).astype(f32)
    for step in range(1, count):
        piece = shifted(block(value, (me + step) % count, count), axis, step)
        total = total + piece.astype(f32)
    return total.astype(value.dtype)


def gather_blocks(value, axis):
    count = lax.axis_size(axis)
    me = lax.axis_index(axis)
    pieces = [value] + [shifted(value, axis, step) for step in range(1, count)]
    out = jnp.zeros((count,) + value.shape, value.dtype)
    for step, piece in enumerate(pieces):
        out = lax.dynamic_update_slice_in_dim(out, piece[None], (me + count - step) % count, 0)
    return out.reshape((-1,) + value.shape[1:])


def kernel_units(values):
    wide = values.astype(f32)
    mean = jnp.sum(wide * wide, axis=1, keepdims=True) * (1.0 / wide.shape[1])
    scale = lax.rsqrt(mean + norm_floor) * (1.0 / wide.shape[1] ** 0.5)
    return (wide * scale).astype(bf16)


def as_row(partials):
    return jnp.sum(partials.T, axis=0, keepdims=True)


def as_column(row):
    return jnp.broadcast_to(row, (LANES, row.shape[1])).T


def column_tile(values, start):
    width = values.shape[1]
    return values[start // width : start // width + 1, start % width : start % width + LANES]


def add_column(ref, start, values):
    width = ref.shape[2]
    tile = (0, slice(start // width, start // width + 1), slice(start % width, start % width + LANES))
    ref[tile] += jnp.sum(values, axis=0, keepdims=True)


def tiles(matrix):
    return range(0, matrix.shape[1], LANES)


def tempered_rows(units, protos_ref, divisor):
    scores = lax.dot_general(
        units, protos_ref[...], (((1,), (1,)), ((), ())), preferred_element_type=f32
    )
    return jnp.exp2(scores * (LOG2_E / divisor))


def steps(count):
    return [slice(start, start + ROWS) for start in range(0, count, ROWS)]


def for_each_receiver(ref):
    for to in range(1, ref.shape[0]):
        ref[to] = ref[0]


def first_kernel(emb_ref, proto_ref, views_ref, protos_ref, col_ref):
    protos_ref[...] = kernel_units(proto_ref[...])
    views_ref[...] = kernel_units(emb_ref[...])
    col_ref[0] = jnp.zeros_like(col_ref[0])

    @pl.loop(0, emb_ref.shape[0] // ROWS)
    def _(step):
        rows = pl.ds(pl.multiple_of(step * ROWS, ROWS), ROWS)
        tempered = tempered_rows(views_ref[rows, :], protos_ref, sharpness_divisor)
        for start in tiles(tempered):
            value = tempered[:, start : start + LANES]
            add_column(col_ref, start, value * value)

    for_each_receiver(col_ref)


def rows_kernel(own, emb_ref, protos_ref, totals_ref, temp_ref, row_ref):
    column_scale = 1.0 / jnp.sum(totals_ref[...], axis=0)

    @pl.loop(0, emb_ref.shape[0] // ROWS)
    def _(step):
        rows = pl.ds(pl.multiple_of(step * ROWS, ROWS), ROWS)
        units = emb_ref[rows, :]
        if own:
            tempered = tempered_rows(units, protos_ref, sharpness_divisor)
        else:
            tempered = tempered_rows(kernel_units(units), protos_ref, epsilon_code)
        temp_ref[rows, :] = tempered
        total = soft = jnp.zeros((ROWS, LANES), f32)
        for start in tiles(tempered):
            value = tempered[:, start : start + LANES]
            if own:
                soft = soft + value
                value = value * value
            total = total + value * column_tile(column_scale, start)
        row_ref[0, :1, rows] = as_row(total)
        if own:
            row_ref[0, 1:, rows] = as_row(soft)

    for_each_receiver(row_ref)


def col_kernel(temp_ref, totals_ref, col_ref):
    weight = 1.0 / jnp.sum(totals_ref[:, 0, :], axis=0, keepdims=True)
    col_ref[0] = jnp.zeros_like(col_ref[0])
    for rows in steps(temp_ref.shape[0]):
        wide = as_column(weight[:, rows])
        for start in tiles(temp_ref):
            value = temp_ref[rows, start : start + LANES]
            add_column(col_ref, start, value * value * wide)
    for_each_receiver(col_ref)


def gradient_kernel(
    other_ref, totals_ref, line_ref, soft_ref, views_ref, protos_ref, view_ref, proto_ref
):
    proto_ref[...] = jnp.zeros_like(proto_ref)
    column_scale = 1.0 / jnp.sum(totals_ref[...], axis=0)
    line_row = 1.0 / jnp.sum(line_ref[:, 0, :], axis=0, keepdims=True)
    soft_row = 1.0 / jnp.sum(soft_ref[:, 1, :], axis=0, keepdims=True)
    for rows in steps(other_ref.shape[0]):
        line = as_column(line_row[:, rows])
        soft = as_column(soft_row[:, rows])
        views = views_ref[rows, :]
        tempered = tempered_rows(views, protos_ref, sharpness_divisor)
        grads = []
        for start in tiles(tempered):
            codes = other_ref[rows, start : start + LANES]
            codes = (codes * column_tile(column_scale, start) * line).astype(bf16)
            likelihood = tempered[:, start : start + LANES] * soft
            grads.append(
                ((likelihood - codes.astype(f32)) * (1.0 / sharpness_divisor)).astype(bf16)
            )
        grad = jnp.concatenate(grads, axis=1)
        view_ref[rows, :] = jnp.dot(grad, protos_ref[...], preferred_element_type=f32)
        proto_ref[...] += lax.dot_general(
            grad, views, (((0,), (0,)), ((), ())), preferred_element_type=f32
        )


def call(kernel, name, ins, outs, flops, size, exps=0):
    in_vmem = pl.BlockSpec(memory_space=pltpu.VMEM)
    return pl.pallas_call(
        kernel,
        name=name,
        out_shape=[jax.ShapeDtypeStruct(shape, kind) for shape, kind in outs],
        in_specs=[in_vmem] * len(ins),
        out_specs=[in_vmem] * len(outs),
        compiler_params=pltpu.CompilerParams(vmem_limit_bytes=16 * 2**20),
        cost_estimate=pl.CostEstimate(flops=flops, bytes_accessed=size, transcendentals=exps),
    )(*ins)


def body(embeddings, prototypes, partner):
    count, width = embeddings.shape
    slots = prototypes.shape[0]
    entries = count * slots
    links = jnp.remainder(partner, count)
    y, z, x, core = (lax.axis_index(name) for name in ("y", "z", "x", "core"))
    y_count, z_count, x_count = (lax.axis_size(name) for name in ("y", "z", "x"))
    matrix, column = (count, slots), (FOLD, slots // FOLD)
    members = 2 * x_count
    own = block(embeddings, x * 2 + core, members)
    sent = shifted(own, "z", z_count // 2)
    views, protos, column_part = call(
        first_kernel,
        "first",
        [embeddings, prototypes],
        [((count, width), bf16), ((slots, width), bf16), ((y_count,) + column, f32)],
        flops=2 * entries * width,
        size=4 * slots * width,
        exps=entries,
    )

    def tempered_pass(mine, rows, totals):
        tempered, part = call(
            functools.partial(rows_kernel, mine),
            "tempered_pass",
            [rows, protos, totals],
            [(matrix, f32), ((members, 2 if mine else 1, count), f32)],
            flops=2 * entries * width,
            size=4 * slots * width,
            exps=entries,
        )
        return tempered, exchanged(part, proto_axes)

    def column_pass(tempered, totals):
        sums = ((y_count,) + column, f32)
        (part,) = call(col_kernel, "column_pass", [tempered, totals], [sums], 3 * entries, 4 * count)
        return total(exchanged(part, "y"))

    sent = gather_blocks(gather_blocks(sent, "core"), "x")
    column_part = total(exchanged(column_part, "y"))
    column_total, sent = lax.optimization_barrier((gathered(column_part, "z"), sent))
    for sweep in range(1, ITERS):
        tempered, row_total = tempered_pass(True, views, column_total)
        column_part = column_pass(tempered, row_total)
        if sweep == ITERS - 1:
            column_part, sent = lax.optimization_barrier((column_part, sent))
        column_total = gathered(column_part, "z")
    other_kernel, line_total = tempered_pass(False, sent[links], column_total)
    view_part, proto_part = call(
        gradient_kernel,
        "gradient",
        [other_kernel, column_total, line_total, row_total, views, protos],
        [((count, width), f32), ((slots, width), f32)],
        flops=6 * entries * width,
        size=8 * slots * width,
        exps=entries,
    )

    proto_rows = unit_rows(block(prototypes, y * z_count + z, y_count * z_count))[0]
    view_rows = unit_rows(block(embeddings, core * x_count + x, members))[0]
    proto_pieces = exchanged(proto_part.astype(SENT).reshape(y_count, -1, width), "y")
    proto_sum = total(proto_pieces).astype(SENT)
    proto_pieces = exchanged(proto_sum.reshape(z_count, -1, width), "z")
    proto_sum = (tangent(total(proto_pieces), proto_rows) * (1.0 / z_count)).astype(SENT)
    proto_sum = gathered(proto_sum, "z").reshape(-1, width)

    view_sum = scatter_sum(scatter_sum(view_part.astype(SENT), "core"), "x")
    view_sum = tangent(view_sum.astype(f32), view_rows).astype(SENT)
    view_sum = gather_blocks(gather_blocks(view_sum, "x"), "core")

    proto_sum = gathered(proto_sum, "y").reshape(slots, width)
    emb_grad = row_scale(embeddings) * view_sum.astype(f32)
    proto_grad = row_scale(prototypes) * float(z_count) * proto_sum.astype(f32)
    return (emb_grad, proto_grad)


def solution(mesh):
    inner = Mesh(mesh.devices.reshape(16, 4, 4, 2), ("z", "y", "x", "core"))
    return jax.shard_map(
        body,
        mesh=inner,
        in_specs=(P(rows_axes, None), P(proto_axes, None), P(rows_axes)),
        out_specs=(P(rows_axes, None), P(proto_axes, None)),
        check_vma=False,
    )
```

```python
import jax
import jax.numpy as jnp
from jax import lax
from jax.experimental import pallas as pl
from jax.experimental.pallas import tpu as pltpu
from jax.sharding import Mesh, PartitionSpec as P

ITERS = 3


epsilon_code = 0.05
sharpness_divisor = 0.1
norm_floor = 1e-06
rows_axes = ("z", "y")
proto_axes = ("x", "core")
LANES = 128
ROWS = 256
f32 = jnp.float32
bf16 = jnp.bfloat16
SENT = jnp.float16
FOLD = 8
LOG2_E = 1.4426950408889634


def shifted(value, axis, steps):
    count = lax.axis_size(axis)
    pairs = [(source, (source + steps) % count) for source in range(count)]
    return lax.ppermute(value, axis, pairs)


def exchanged(value, axis):
    return lax.all_to_all(value, axis, 0, 0, tiled=True)


def gathered(value, axis):
    return exchanged(jnp.broadcast_to(value[None], (lax.axis_size(axis),) + value.shape), axis)


def unit_rows(values):
    wide = values.astype(f32)
    scale = lax.rsqrt(jnp.mean(wide * wide, axis=1, keepdims=True) + norm_floor) / jnp.sqrt(
        f32(wide.shape[1])
    )
    return (wide * scale, scale)


def row_scale(values):
    return unit_rows(values)[1]


def tangent(upstream, units):
    return upstream - units * jnp.sum(units * upstream, axis=1, keepdims=True)


def total(pieces):
    parts = [pieces[index].astype(f32) for index in range(pieces.shape[0])]
    while len(parts) > 1:
        parts = [left + right for left, right in zip(parts[::2], parts[1::2], strict=True)]
    return parts[0]


def block(value, index, count):
    size = value.shape[0] // count
    return lax.dynamic_slice_in_dim(value, index * size, size, 0)


def scatter_sum(value, axis):
    count = lax.axis_size(axis)
    me = lax.axis_index(axis)
    total = block(value, me, count).astype(f32)
    for step in range(1, count):
        piece = shifted(block(value, (me + step) % count, count), axis, step)
        total = total + piece.astype(f32)
    return total.astype(value.dtype)


def gather_blocks(value, axis):
    count = lax.axis_size(axis)
    me = lax.axis_index(axis)
    pieces = [value] + [shifted(value, axis, step) for step in range(1, count)]
    out = jnp.zeros((count,) + value.shape, value.dtype)
    for step, piece in enumerate(pieces):
        out = lax.dynamic_update_slice_in_dim(out, piece[None], (me + count - step) % count, 0)
    return out.reshape((-1,) + value.shape[1:])


def kernel_units(values):
    wide = values.astype(f32)
    mean = jnp.sum(wide * wide, axis=1, keepdims=True) * (1.0 / wide.shape[1])
    scale = lax.rsqrt(mean + norm_floor) * (1.0 / wide.shape[1] ** 0.5)
    return (wide * scale).astype(bf16)


def as_row(partials):
    return jnp.sum(partials.T, axis=0, keepdims=True)


def as_column(row):
    return jnp.broadcast_to(row, (LANES, row.shape[1])).T


def column_tile(values, start):
    width = values.shape[1]
    return values[start // width : start // width + 1, start % width : start % width + LANES]


def add_column(ref, start, values):
    width = ref.shape[2]
    tile = (0, slice(start // width, start // width + 1), slice(start % width, start % width + LANES))
    ref[tile] += jnp.sum(values, axis=0, keepdims=True)


def tiles(matrix):
    return range(0, matrix.shape[1], LANES)


def tempered_rows(units, protos_ref, divisor):
    scores = lax.dot_general(
        units, protos_ref[...], (((1,), (1,)), ((), ())), preferred_element_type=f32
    )
    return jnp.exp2(scores * (LOG2_E / divisor))


def steps(count):
    return [slice(start, start + ROWS) for start in range(0, count, ROWS)]


def for_each_receiver(ref):
    for to in range(1, ref.shape[0]):
        ref[to] = ref[0]


def first_kernel(emb_ref, proto_ref, views_ref, protos_ref, col_ref):
    protos_ref[...] = kernel_units(proto_ref[...])
    views_ref[...] = kernel_units(emb_ref[...])
    col_ref[0] = jnp.zeros_like(col_ref[0])

    @pl.loop(0, emb_ref.shape[0] // ROWS)
    def _(step):
        rows = pl.ds(pl.multiple_of(step * ROWS, ROWS), ROWS)
        tempered = tempered_rows(views_ref[rows, :], protos_ref, sharpness_divisor)
        for start in tiles(tempered):
            value = tempered[:, start : start + LANES]
            add_column(col_ref, start, value * value)

    for_each_receiver(col_ref)


def rows_kernel(views_ref, protos_ref, totals_ref, temp_ref, row_ref):
    column_scale = 1.0 / jnp.sum(totals_ref[...].astype(f32), axis=0)

    @pl.loop(0, views_ref.shape[0] // ROWS)
    def _(step):
        rows = pl.ds(pl.multiple_of(step * ROWS, ROWS), ROWS)
        tempered = tempered_rows(views_ref[rows, :], protos_ref, sharpness_divisor)
        temp_ref[rows, :] = tempered
        total = soft = jnp.zeros((ROWS, LANES), f32)
        for start in tiles(tempered):
            value = tempered[:, start : start + LANES]
            soft = soft + value
            total = total + value * value * column_tile(column_scale, start)
        row_ref[0, :1, rows] = as_row(total)
        row_ref[0, 1:, rows] = as_row(soft)

    for_each_receiver(row_ref)


def line_kernel(views_ref, protos_ref, totals_ref, kernel_ref, row_ref):
    column_scale = 1.0 / jnp.sum(totals_ref[...], axis=0)

    @pl.loop(0, views_ref.shape[0] // ROWS)
    def _(step):
        rows = pl.ds(pl.multiple_of(step * ROWS, ROWS), ROWS)
        kernel = tempered_rows(views_ref[rows, :], protos_ref, epsilon_code)
        kernel_ref[rows, :] = kernel
        total = jnp.zeros((ROWS, LANES), f32)
        for start in tiles(kernel):
            total = total + kernel[:, start : start + LANES] * column_tile(column_scale, start)
        row_ref[0, :, rows] = as_row(total)

    for_each_receiver(row_ref)


def col_kernel(temp_ref, totals_ref, col_ref):
    weight = 1.0 / jnp.sum(totals_ref[:, 0, :], axis=0, keepdims=True)
    col_ref[0] = jnp.zeros_like(col_ref[0])
    for rows in steps(temp_ref.shape[0]):
        wide = as_column(weight[:, rows])
        for start in tiles(temp_ref):
            value = temp_ref[rows, start : start + LANES]
            add_column(col_ref, start, value * value * wide)
    for_each_receiver(col_ref)


def gradient_kernel(
    other_ref, totals_ref, line_ref, soft_ref, views_ref, protos_ref, view_ref, proto_ref
):
    proto_ref[...] = jnp.zeros_like(proto_ref)
    column_scale = 1.0 / jnp.sum(totals_ref[...], axis=0)
    line_row = 1.0 / jnp.sum(line_ref[:, 0, :], axis=0, keepdims=True)
    soft_row = 1.0 / jnp.sum(soft_ref[:, 1, :], axis=0, keepdims=True)
    for rows in steps(other_ref.shape[0]):
        line = as_column(line_row[:, rows])
        soft = as_column(soft_row[:, rows])
        views = views_ref[rows, :]
        tempered = tempered_rows(views, protos_ref, sharpness_divisor)
        grads = []
        for start in tiles(tempered):
            codes = other_ref[rows, start : start + LANES]
            codes = (codes * column_tile(column_scale, start) * line).astype(bf16)
            likelihood = tempered[:, start : start + LANES] * soft
            grads.append(
                ((likelihood - codes.astype(f32)) * (1.0 / sharpness_divisor)).astype(bf16)
            )
        grad = jnp.concatenate(grads, axis=1)
        view_ref[rows, :] = jnp.dot(grad, protos_ref[...], preferred_element_type=f32)
        proto_ref[...] += lax.dot_general(
            grad, views, (((0,), (0,)), ((), ())), preferred_element_type=f32
        )


def call(kernel, name, ins, outs, flops, size, exps=0):
    in_vmem = pl.BlockSpec(memory_space=pltpu.VMEM)
    return pl.pallas_call(
        kernel,
        name=name,
        out_shape=[jax.ShapeDtypeStruct(shape, kind) for shape, kind in outs],
        in_specs=[in_vmem] * len(ins),
        out_specs=[in_vmem] * len(outs),
        compiler_params=pltpu.CompilerParams(vmem_limit_bytes=16 * 2**20),
        cost_estimate=pl.CostEstimate(flops=flops, bytes_accessed=size, transcendentals=exps),
    )(*ins)


def body(embeddings, prototypes, partner):
    count, width = embeddings.shape
    slots = prototypes.shape[0]
    entries = count * slots
    links = jnp.remainder(partner, count)
    y, z, x, core = (lax.axis_index(name) for name in ("y", "z", "x", "core"))
    y_count, z_count, x_count = (lax.axis_size(name) for name in ("y", "z", "x"))
    matrix, column = (count, slots), (FOLD, slots // FOLD)
    members = 2 * x_count
    own = block(embeddings, x * 2 + core, members)
    sent = shifted(own, "z", z_count // 2)
    views, protos, column_part = call(
        first_kernel,
        "first",
        [embeddings, prototypes],
        [((count, width), bf16), ((slots, width), bf16), ((y_count,) + column, f32)],
        flops=2 * entries * width,
        size=4 * slots * width,
        exps=entries,
    )

    def tempered_pass(rows, totals):
        tempered, part = call(
            rows_kernel,
            "tempered_pass",
            [rows, protos, totals],
            [(matrix, f32), ((members, 2, count), f32)],
            flops=2 * entries * width,
            size=4 * slots * width,
            exps=entries,
        )
        return tempered, exchanged(part, proto_axes)

    def column_pass(tempered, totals):
        sums = ((y_count,) + column, f32)
        (part,) = call(col_kernel, "column_pass", [tempered, totals], [sums], 3 * entries, 4 * count)
        return total(exchanged(part, "y"))

    sent = gather_blocks(gather_blocks(sent, "core"), "x")
    column_part = total(exchanged(column_part, "y"))
    column_total = gathered(column_part.astype(bf16), "z")
    column_total, sent = lax.optimization_barrier((column_total, sent))
    tempered, row_total = tempered_pass(views, column_total)
    column_part, sent = lax.optimization_barrier((column_pass(tempered, row_total), sent))
    other = sent[links]
    column_total = gathered(column_part.astype(bf16), "z")
    for sweep in range(2, ITERS):
        column_total, other = lax.optimization_barrier((column_total, other))
        tempered, row_total = tempered_pass(views, column_total)
        column_part, other = lax.optimization_barrier((column_pass(tempered, row_total), other))
        column_total = gathered(column_part, "z")
    other_views = unit_rows(other)[0].astype(bf16)
    other_kernel, line_part = call(
        line_kernel,
        "lines",
        [other_views, protos, column_total],
        [(matrix, f32), ((members, 1, count), f32)],
        flops=2 * entries * width,
        size=4 * slots * width,
        exps=entries,
    )
    line_total = exchanged(line_part, proto_axes)
    view_part, proto_part = call(
        gradient_kernel,
        "gradient",
        [other_kernel, column_total, line_total, row_total, views, protos],
        [((count, width), f32), ((slots, width), f32)],
        flops=6 * entries * width,
        size=8 * slots * width,
        exps=entries,
    )

    proto_rows = unit_rows(block(prototypes, y * z_count + z, y_count * z_count))[0]
    view_rows = unit_rows(block(embeddings, core * x_count + x, members))[0]
    proto_pieces = exchanged(proto_part.astype(SENT).reshape(y_count, -1, width), "y")
    proto_sum = total(proto_pieces).astype(SENT)
    proto_pieces = exchanged(proto_sum.reshape(z_count, -1, width), "z")
    proto_sum = (tangent(total(proto_pieces), proto_rows) * (1.0 / z_count)).astype(SENT)
    proto_sum = gathered(proto_sum, "z").reshape(-1, width)

    view_sum = scatter_sum(scatter_sum(view_part.astype(SENT), "core"), "x")
    view_sum = tangent(view_sum.astype(f32), view_rows).astype(SENT)
    view_sum = gather_blocks(gather_blocks(view_sum, "x"), "core")

    proto_sum = gathered(proto_sum, "y").reshape(slots, width)
    emb_grad = row_scale(embeddings) * view_sum.astype(f32)
    proto_grad = row_scale(prototypes) * float(z_count) * proto_sum.astype(f32)
    return (emb_grad, proto_grad)


def solution(mesh):
    inner = Mesh(mesh.devices.reshape(16, 4, 4, 2), ("z", "y", "x", "core"))
    return jax.shard_map(
        body,
        mesh=inner,
        in_specs=(P(rows_axes, None), P(proto_axes, None), P(rows_axes)),
        out_specs=(P(rows_axes, None), P(proto_axes, None)),
        check_vma=False,
    )
```

```python
import jax
import jax.numpy as jnp
from jax import lax
from jax.experimental import pallas as pl
from jax.experimental.pallas import tpu as pltpu
from jax.sharding import Mesh, PartitionSpec as P

ITERS = 3


epsilon_code = 0.05
sharpness_divisor = 0.1
norm_floor = 1e-06
rows_axes = ("z", "y")
proto_axes = ("x", "core")
LANES = 128
ROWS = 256
f32 = jnp.float32
bf16 = jnp.bfloat16
SENT = jnp.float16
FOLD = 8
LOG2_E = 1.4426950408889634


def shifted(value, axis, steps):
    count = lax.axis_size(axis)
    pairs = [(source, (source + steps) % count) for source in range(count)]
    return lax.ppermute(value, axis, pairs)


def exchanged(value, axis):
    return lax.all_to_all(value, axis, 0, 0, tiled=True)


def gathered(value, axis):
    return exchanged(jnp.broadcast_to(value[None], (lax.axis_size(axis),) + value.shape), axis)


def unit_rows(values):
    wide = values.astype(f32)
    scale = lax.rsqrt(jnp.mean(wide * wide, axis=1, keepdims=True) + norm_floor) / jnp.sqrt(
        f32(wide.shape[1])
    )
    return (wide * scale, scale)


def row_scale(values):
    return unit_rows(values)[1]


def tangent(upstream, units):
    return upstream - units * jnp.sum(units * upstream, axis=1, keepdims=True)


def total(pieces):
    parts = [pieces[index].astype(f32) for index in range(pieces.shape[0])]
    while len(parts) > 1:
        parts = [left + right for left, right in zip(parts[::2], parts[1::2], strict=True)]
    return parts[0]


def block(value, index, count):
    size = value.shape[0] // count
    return lax.dynamic_slice_in_dim(value, index * size, size, 0)


def scatter_sum(value, axis):
    count = lax.axis_size(axis)
    me = lax.axis_index(axis)
    total = block(value, me, count).astype(f32)
    for step in range(1, count):
        piece = shifted(block(value, (me + step) % count, count), axis, step)
        total = total + piece.astype(f32)
    return total.astype(value.dtype)


def gather_blocks(value, axis):
    count = lax.axis_size(axis)
    me = lax.axis_index(axis)
    pieces = [value] + [shifted(value, axis, step) for step in range(1, count)]
    out = jnp.zeros((count,) + value.shape, value.dtype)
    for step, piece in enumerate(pieces):
        out = lax.dynamic_update_slice_in_dim(out, piece[None], (me + count - step) % count, 0)
    return out.reshape((-1,) + value.shape[1:])


def kernel_units(values):
    wide = values.astype(f32)
    mean = jnp.sum(wide * wide, axis=1, keepdims=True) * (1.0 / wide.shape[1])
    scale = lax.rsqrt(mean + norm_floor) * (1.0 / wide.shape[1] ** 0.5)
    return (wide * scale).astype(bf16)


def as_row(partials):
    return jnp.sum(partials.T, axis=0, keepdims=True)


def as_column(row):
    return jnp.broadcast_to(row, (LANES, row.shape[1])).T


def column_tile(values, start):
    width = values.shape[1]
    return values[start // width : start // width + 1, start % width : start % width + LANES]


def add_column(ref, start, values):
    width = ref.shape[2]
    tile = (0, slice(start // width, start // width + 1), slice(start % width, start % width + LANES))
    ref[tile] += jnp.sum(values, axis=0, keepdims=True)


def tiles(matrix):
    return range(0, matrix.shape[1], LANES)


def tempered_rows(units, protos_ref, divisor):
    scores = lax.dot_general(
        units, protos_ref[...], (((1,), (1,)), ((), ())), preferred_element_type=f32
    )
    return jnp.exp2(scores * (LOG2_E / divisor))


def steps(count):
    return [slice(start, start + ROWS) for start in range(0, count, ROWS)]


def for_each_receiver(ref):
    for to in range(1, ref.shape[0]):
        ref[to] = ref[0]


def first_kernel(emb_ref, proto_ref, views_ref, protos_ref, col_ref):
    protos_ref[...] = kernel_units(proto_ref[...])
    views_ref[...] = kernel_units(emb_ref[...])
    col_ref[0] = jnp.zeros_like(col_ref[0])

    @pl.loop(0, emb_ref.shape[0] // ROWS)
    def _(step):
        rows = pl.ds(pl.multiple_of(step * ROWS, ROWS), ROWS)
        tempered = tempered_rows(views_ref[rows, :], protos_ref, sharpness_divisor)
        for start in tiles(tempered):
            value = tempered[:, start : start + LANES]
            add_column(col_ref, start, value * value)

    for_each_receiver(col_ref)


def rows_kernel(views_ref, protos_ref, totals_ref, temp_ref, row_ref):
    column_scale = 1.0 / jnp.sum(totals_ref[...].astype(f32), axis=0)

    @pl.loop(0, views_ref.shape[0] // ROWS)
    def _(step):
        rows = pl.ds(pl.multiple_of(step * ROWS, ROWS), ROWS)
        tempered = tempered_rows(views_ref[rows, :], protos_ref, sharpness_divisor)
        temp_ref[rows, :] = tempered
        total = soft = jnp.zeros((ROWS, LANES), f32)
        for start in tiles(tempered):
            value = tempered[:, start : start + LANES]
            soft = soft + value
            total = total + value * value * column_tile(column_scale, start)
        row_ref[0, :1, rows] = as_row(total)
        row_ref[0, 1:, rows] = as_row(soft)

    for_each_receiver(row_ref)


def line_kernel(views_ref, protos_ref, totals_ref, kernel_ref, row_ref):
    column_scale = 1.0 / jnp.sum(totals_ref[...], axis=0)

    @pl.loop(0, views_ref.shape[0] // ROWS)
    def _(step):
        rows = pl.ds(pl.multiple_of(step * ROWS, ROWS), ROWS)
        kernel = tempered_rows(views_ref[rows, :], protos_ref, epsilon_code)
        kernel_ref[rows, :] = kernel
        total = jnp.zeros((ROWS, LANES), f32)
        for start in tiles(kernel):
            total = total + kernel[:, start : start + LANES] * column_tile(column_scale, start)
        row_ref[0, :, rows] = as_row(total)

    for_each_receiver(row_ref)


def col_kernel(temp_ref, totals_ref, col_ref):
    weight = 1.0 / jnp.sum(totals_ref[:, 0, :], axis=0, keepdims=True)
    col_ref[0] = jnp.zeros_like(col_ref[0])
    for rows in steps(temp_ref.shape[0]):
        wide = as_column(weight[:, rows])
        for start in tiles(temp_ref):
            value = temp_ref[rows, start : start + LANES]
            add_column(col_ref, start, value * value * wide)
    for_each_receiver(col_ref)


def gradient_kernel(
    other_ref, totals_ref, line_ref, soft_ref, views_ref, protos_ref, view_ref, proto_ref
):
    proto_ref[...] = jnp.zeros_like(proto_ref)
    column_scale = 1.0 / jnp.sum(totals_ref[...], axis=0)
    line_row = 1.0 / jnp.sum(line_ref[:, 0, :], axis=0, keepdims=True)
    soft_row = 1.0 / jnp.sum(soft_ref[:, 1, :], axis=0, keepdims=True)
    for rows in steps(other_ref.shape[0]):
        line = as_column(line_row[:, rows])
        soft = as_column(soft_row[:, rows])
        views = views_ref[rows, :]
        tempered = tempered_rows(views, protos_ref, sharpness_divisor)
        grads = []
        for start in tiles(tempered):
            codes = other_ref[rows, start : start + LANES]
            codes = (codes * column_tile(column_scale, start) * line).astype(bf16)
            likelihood = tempered[:, start : start + LANES] * soft
            grads.append(
                ((likelihood - codes.astype(f32)) * (1.0 / sharpness_divisor)).astype(bf16)
            )
        grad = jnp.concatenate(grads, axis=1)
        view_ref[rows, :] = jnp.dot(grad, protos_ref[...], preferred_element_type=f32)
        proto_ref[...] += lax.dot_general(
            grad, views, (((0,), (0,)), ((), ())), preferred_element_type=f32
        )


def call(kernel, name, ins, outs, flops, size, exps=0):
    in_vmem = pl.BlockSpec(memory_space=pltpu.VMEM)
    return pl.pallas_call(
        kernel,
        name=name,
        out_shape=[jax.ShapeDtypeStruct(shape, kind) for shape, kind in outs],
        in_specs=[in_vmem] * len(ins),
        out_specs=[in_vmem] * len(outs),
        compiler_params=pltpu.CompilerParams(vmem_limit_bytes=16 * 2**20),
        cost_estimate=pl.CostEstimate(flops=flops, bytes_accessed=size, transcendentals=exps),
    )(*ins)


def body(embeddings, prototypes, partner):
    count, width = embeddings.shape
    slots = prototypes.shape[0]
    entries = count * slots
    links = jnp.remainder(partner, count)
    y, z, x, core = (lax.axis_index(name) for name in ("y", "z", "x", "core"))
    y_count, z_count, x_count = (lax.axis_size(name) for name in ("y", "z", "x"))
    matrix, column = (count, slots), (FOLD, slots // FOLD)
    members = 2 * x_count
    own = block(embeddings, x * 2 + core, members)
    sent = shifted(own, "z", z_count // 2)
    views, protos, column_part = call(
        first_kernel,
        "first",
        [embeddings, prototypes],
        [((count, width), bf16), ((slots, width), bf16), ((y_count,) + column, f32)],
        flops=2 * entries * width,
        size=4 * slots * width,
        exps=entries,
    )

    def tempered_pass(rows, totals):
        tempered, part = call(
            rows_kernel,
            "tempered_pass",
            [rows, protos, totals],
            [(matrix, f32), ((members, 2, count), f32)],
            flops=2 * entries * width,
            size=4 * slots * width,
            exps=entries,
        )
        return tempered, exchanged(part, proto_axes)

    def column_pass(tempered, totals):
        sums = ((y_count,) + column, f32)
        (part,) = call(col_kernel, "column_pass", [tempered, totals], [sums], 3 * entries, 4 * count)
        return total(exchanged(part, "y"))

    sent = gather_blocks(gather_blocks(sent, "core"), "x")
    column_part = total(exchanged(column_part, "y"))
    column_total = gathered(column_part.astype(bf16), "z")
    column_total, sent = lax.optimization_barrier((column_total, sent))
    tempered, row_total = tempered_pass(views, column_total)
    column_part, sent = lax.optimization_barrier((column_pass(tempered, row_total), sent))
    other = sent[links]
    column_total = gathered(column_part.astype(bf16), "z")
    for sweep in range(2, ITERS):
        column_total, other = lax.optimization_barrier((column_total, other))
        tempered, row_total = tempered_pass(views, column_total)
        column_part, other = lax.optimization_barrier((column_pass(tempered, row_total), other))
        column_total = gathered(column_part, "z")
    other_views = unit_rows(other)[0].astype(bf16)
    other_kernel, line_part = call(
        line_kernel,
        "lines",
        [other_views, protos, column_total],
        [(matrix, f32), ((members, 1, count), f32)],
        flops=2 * entries * width,
        size=4 * slots * width,
        exps=entries,
    )
    line_total = exchanged(line_part, proto_axes)
    view_part, proto_part = call(
        gradient_kernel,
        "gradient",
        [other_kernel, column_total, line_total, row_total, views, protos],
        [((count, width), f32), ((slots, width), f32)],
        flops=6 * entries * width,
        size=8 * slots * width,
        exps=entries,
    )

    proto_rows = unit_rows(block(prototypes, y * z_count + z, y_count * z_count))[0]
    view_rows = unit_rows(block(embeddings, core * x_count + x, members))[0]
    proto_pieces = exchanged(proto_part.astype(SENT).reshape(y_count, -1, width), "y")
    proto_sum = total(proto_pieces).astype(SENT)
    proto_pieces = exchanged(proto_sum.reshape(z_count, -1, width), "z")
    proto_sum = (tangent(total(proto_pieces), proto_rows) * (1.0 / z_count)).astype(SENT)
    proto_sum = gathered(proto_sum, "z").reshape(-1, width)

    view_sum = scatter_sum(scatter_sum(view_part.astype(SENT), "core"), "x")
    view_sum = tangent(view_sum.astype(f32), view_rows).astype(SENT)
    view_sum = gather_blocks(gather_blocks(view_sum, "x"), "core")

    emb_grad = row_scale(embeddings) * view_sum.astype(f32)
    proto_scale = row_scale(prototypes) * float(z_count)

    proto_sum, emb_grad, proto_scale = lax.optimization_barrier((proto_sum, emb_grad, proto_scale))
    proto_sum = gathered(proto_sum, "y").reshape(slots, width)
    proto_grad = proto_scale * proto_sum.astype(f32)
    return (emb_grad, proto_grad)


def solution(mesh):
    inner = Mesh(mesh.devices.reshape(16, 4, 4, 2), ("z", "y", "x", "core"))
    return jax.shard_map(
        body,
        mesh=inner,
        in_specs=(P(rows_axes, None), P(proto_axes, None), P(rows_axes)),
        out_specs=(P(rows_axes, None), P(proto_axes, None)),
        check_vma=False,
    )
```

```python
import jax
import jax.numpy as jnp
from jax import lax
from jax.experimental import pallas as pl
from jax.experimental.pallas import tpu as pltpu
from jax.sharding import Mesh, PartitionSpec as P

ITERS = 3


epsilon_code = 0.05
sharpness_divisor = 0.1
norm_floor = 1e-06
rows_axes = ("z", "y")
proto_axes = ("x", "core")
LANES = 128
ROWS = 256
f32 = jnp.float32
bf16 = jnp.bfloat16
SENT = jnp.float16
FOLD = 8
LOG2_E = 1.4426950408889634


def shifted(value, axis, steps):
    count = lax.axis_size(axis)
    pairs = [(source, (source + steps) % count) for source in range(count)]
    return lax.ppermute(value, axis, pairs)


def exchanged(value, axis):
    return lax.all_to_all(value, axis, 0, 0, tiled=True)


def gathered(value, axis):
    return exchanged(jnp.broadcast_to(value[None], (lax.axis_size(axis),) + value.shape), axis)


def unit_rows(values):
    wide = values.astype(f32)
    scale = lax.rsqrt(jnp.mean(wide * wide, axis=1, keepdims=True) + norm_floor) / jnp.sqrt(
        f32(wide.shape[1])
    )
    return (wide * scale, scale)


def row_scale(values):
    return unit_rows(values)[1]


def tangent(upstream, units):
    return upstream - units * jnp.sum(units * upstream, axis=1, keepdims=True)


def total(pieces):
    parts = [pieces[index].astype(f32) for index in range(pieces.shape[0])]
    while len(parts) > 1:
        parts = [left + right for left, right in zip(parts[::2], parts[1::2], strict=True)]
    return parts[0]


def block(value, index, count):
    size = value.shape[0] // count
    return lax.dynamic_slice_in_dim(value, index * size, size, 0)


def scatter_sum(value, axis, me):
    count = lax.axis_size(axis)
    total = block(value, me, count).astype(f32)
    for step in range(1, count):
        piece = shifted(block(value, (me + step) % count, count), axis, step)
        total = total + piece.astype(f32)
    return total.astype(value.dtype)


def gather_blocks(value, axis, me):
    count = lax.axis_size(axis)
    out = jnp.broadcast_to(value[None], (count,) + value.shape)
    for step in range(1, count):
        piece = shifted(value, axis, step)[None]
        out = lax.dynamic_update_slice_in_dim(out, piece, (me + count - step) % count, 0)
    return out.reshape((-1,) + value.shape[1:])


def kernel_units(values):
    wide = values.astype(f32)
    mean = jnp.sum(wide * wide, axis=1, keepdims=True) * (1.0 / wide.shape[1])
    scale = lax.rsqrt(mean + norm_floor) * (1.0 / wide.shape[1] ** 0.5)
    return (wide * scale).astype(bf16)


def as_row(partials):
    return jnp.sum(partials.T, axis=0, keepdims=True)


def as_column(row):
    return jnp.broadcast_to(row, (LANES, row.shape[1])).T


def column_tile(values, start):
    width = values.shape[1]
    return values[start // width : start // width + 1, start % width : start % width + LANES]


def add_column(ref, start, values):
    width = ref.shape[2]
    tile = (0, slice(start // width, start // width + 1), slice(start % width, start % width + LANES))
    ref[tile] += jnp.sum(values, axis=0, keepdims=True)


def tiles(matrix):
    return range(0, matrix.shape[1], LANES)


def tempered_rows(units, protos_ref, divisor):
    scores = lax.dot_general(
        units, protos_ref[...], (((1,), (1,)), ((), ())), preferred_element_type=f32
    )
    return jnp.exp2(scores * (LOG2_E / divisor))


def steps(count):
    return [slice(start, start + ROWS) for start in range(0, count, ROWS)]


def for_each_receiver(ref):
    for to in range(1, ref.shape[0]):
        ref[to] = ref[0]


def first_kernel(emb_ref, proto_ref, views_ref, protos_ref, col_ref):
    protos_ref[...] = kernel_units(proto_ref[...])
    views_ref[...] = kernel_units(emb_ref[...])
    col_ref[0] = jnp.zeros_like(col_ref[0])

    @pl.loop(0, emb_ref.shape[0] // ROWS)
    def _(step):
        rows = pl.ds(pl.multiple_of(step * ROWS, ROWS), ROWS)
        tempered = tempered_rows(views_ref[rows, :], protos_ref, sharpness_divisor)
        for start in tiles(tempered):
            value = tempered[:, start : start + LANES]
            add_column(col_ref, start, value * value)

    for_each_receiver(col_ref)


def rows_kernel(views_ref, protos_ref, totals_ref, temp_ref, row_ref):
    column_scale = 1.0 / jnp.sum(totals_ref[...].astype(f32), axis=0)

    @pl.loop(0, views_ref.shape[0] // ROWS)
    def _(step):
        rows = pl.ds(pl.multiple_of(step * ROWS, ROWS), ROWS)
        tempered = tempered_rows(views_ref[rows, :], protos_ref, sharpness_divisor)
        temp_ref[rows, :] = tempered
        total = soft = jnp.zeros((ROWS, LANES), f32)
        for start in tiles(tempered):
            value = tempered[:, start : start + LANES]
            soft = soft + value
            total = total + value * value * column_tile(column_scale, start)
        row_ref[0, :1, rows] = as_row(total)
        row_ref[0, 1:, rows] = as_row(soft)

    for_each_receiver(row_ref)


def line_kernel(views_ref, protos_ref, totals_ref, kernel_ref, row_ref):
    column_scale = 1.0 / jnp.sum(totals_ref[...], axis=0)

    @pl.loop(0, views_ref.shape[0] // ROWS)
    def _(step):
        rows = pl.ds(pl.multiple_of(step * ROWS, ROWS), ROWS)
        kernel = tempered_rows(views_ref[rows, :], protos_ref, epsilon_code)
        kernel_ref[rows, :] = kernel
        total = jnp.zeros((ROWS, LANES), f32)
        for start in tiles(kernel):
            total = total + kernel[:, start : start + LANES] * column_tile(column_scale, start)
        row_ref[0, :, rows] = as_row(total)

    for_each_receiver(row_ref)


def col_kernel(temp_ref, totals_ref, col_ref):
    weight = 1.0 / jnp.sum(totals_ref[:, 0, :], axis=0, keepdims=True)
    col_ref[0] = jnp.zeros_like(col_ref[0])
    for rows in steps(temp_ref.shape[0]):
        wide = as_column(weight[:, rows])
        for start in tiles(temp_ref):
            value = temp_ref[rows, start : start + LANES]
            add_column(col_ref, start, value * value * wide)
    for_each_receiver(col_ref)


def gradient_kernel(
    other_ref, totals_ref, line_ref, soft_ref, views_ref, protos_ref, view_ref, proto_ref
):
    proto_ref[...] = jnp.zeros_like(proto_ref)
    column_scale = 1.0 / jnp.sum(totals_ref[...], axis=0)
    line_row = 1.0 / jnp.sum(line_ref[:, 0, :], axis=0, keepdims=True)
    soft_row = 1.0 / jnp.sum(soft_ref[:, 1, :], axis=0, keepdims=True)
    for rows in steps(other_ref.shape[0]):
        line = as_column(line_row[:, rows])
        soft = as_column(soft_row[:, rows])
        views = views_ref[rows, :]
        tempered = tempered_rows(views, protos_ref, sharpness_divisor)
        grads = []
        for start in tiles(tempered):
            codes = other_ref[rows, start : start + LANES]
            codes = (codes * column_tile(column_scale, start) * line).astype(bf16)
            likelihood = tempered[:, start : start + LANES] * soft
            grads.append(
                ((likelihood - codes.astype(f32)) * (1.0 / sharpness_divisor)).astype(bf16)
            )
        grad = jnp.concatenate(grads, axis=1)
        view_ref[rows, :] = jnp.dot(grad, protos_ref[...], preferred_element_type=f32)
        proto_ref[...] += lax.dot_general(
            grad, views, (((0,), (0,)), ((), ())), preferred_element_type=f32
        )


def call(kernel, name, ins, outs, flops, size, exps=0):
    in_vmem = pl.BlockSpec(memory_space=pltpu.VMEM)
    return pl.pallas_call(
        kernel,
        name=name,
        out_shape=[jax.ShapeDtypeStruct(shape, kind) for shape, kind in outs],
        in_specs=[in_vmem] * len(ins),
        out_specs=[in_vmem] * len(outs),
        compiler_params=pltpu.CompilerParams(vmem_limit_bytes=16 * 2**20),
        cost_estimate=pl.CostEstimate(flops=flops, bytes_accessed=size, transcendentals=exps),
    )(*ins)


def body(embeddings, prototypes, partner):
    count, width = embeddings.shape
    slots = prototypes.shape[0]
    entries = count * slots
    links = jnp.remainder(partner, count)
    y, z, x, core = (lax.axis_index(name) for name in ("y", "z", "x", "core"))
    y_count, z_count, x_count = (lax.axis_size(name) for name in ("y", "z", "x"))
    matrix, column = (count, slots), (FOLD, slots // FOLD)
    members = 2 * x_count
    own = block(embeddings, x * 2 + core, members)
    sent = shifted(own, "z", z_count // 2)
    views, protos, column_part = call(
        first_kernel,
        "first",
        [embeddings, prototypes],
        [((count, width), bf16), ((slots, width), bf16), ((y_count,) + column, f32)],
        flops=2 * entries * width,
        size=4 * slots * width,
        exps=entries,
    )

    def tempered_pass(rows, totals):
        tempered, part = call(
            rows_kernel,
            "tempered_pass",
            [rows, protos, totals],
            [(matrix, f32), ((members, 2, count), f32)],
            flops=2 * entries * width,
            size=4 * slots * width,
            exps=entries,
        )
        return tempered, exchanged(part, proto_axes)

    def column_pass(tempered, totals):
        sums = ((y_count,) + column, f32)
        (part,) = call(col_kernel, "column_pass", [tempered, totals], [sums], 3 * entries, 4 * count)
        return total(exchanged(part, "y"))

    sent = gather_blocks(gather_blocks(sent, "core", core), "x", x)
    column_part = total(exchanged(column_part, "y"))
    column_total = gathered(column_part.astype(bf16), "z")
    column_total, sent, place = lax.optimization_barrier((column_total, sent, (y, z, x, core)))
    tempered, row_total = tempered_pass(views, column_total)
    column_part, sent = lax.optimization_barrier((column_pass(tempered, row_total), sent))
    other = sent[links]
    column_total = gathered(column_part.astype(bf16), "z")
    for sweep in range(2, ITERS):
        column_total, other = lax.optimization_barrier((column_total, other))
        tempered, row_total = tempered_pass(views, column_total)
        column_part, other = lax.optimization_barrier((column_pass(tempered, row_total), other))
        column_total = gathered(column_part, "z")
    other_views = unit_rows(other)[0].astype(bf16)
    other_kernel, line_part = call(
        line_kernel,
        "lines",
        [other_views, protos, column_total],
        [(matrix, f32), ((members, 1, count), f32)],
        flops=2 * entries * width,
        size=4 * slots * width,
        exps=entries,
    )
    line_total = exchanged(line_part, proto_axes)
    view_part, proto_part = call(
        gradient_kernel,
        "gradient",
        [other_kernel, column_total, line_total, row_total, views, protos],
        [((count, width), f32), ((slots, width), f32)],
        flops=6 * entries * width,
        size=8 * slots * width,
        exps=entries,
    )

    view_part, proto_part, late_emb, late_proto, (y, z, x, core) = lax.optimization_barrier(
        (view_part, proto_part, embeddings, prototypes, place)
    )
    proto_rows = unit_rows(block(late_proto, y * z_count + z, y_count * z_count))[0]
    view_rows = unit_rows(block(late_emb, core * x_count + x, members))[0]
    proto_pieces = exchanged(proto_part.astype(SENT).reshape(y_count, -1, width), "y")
    proto_sum = total(proto_pieces).astype(SENT)
    proto_pieces = exchanged(proto_sum.reshape(z_count, -1, width), "z")
    proto_sum = (tangent(total(proto_pieces), proto_rows) * (1.0 / z_count)).astype(SENT)
    proto_sum = gathered(proto_sum, "z").reshape(-1, width)

    view_sum = scatter_sum(scatter_sum(view_part.astype(SENT), "core", core), "x", x)
    view_sum = tangent(view_sum.astype(f32), view_rows).astype(SENT)
    view_sum = gather_blocks(gather_blocks(view_sum, "x", x), "core", core)

    emb_grad = row_scale(late_emb) * view_sum.astype(f32)
    proto_scale = row_scale(late_proto) * float(z_count)

    proto_sum, emb_grad, proto_scale = lax.optimization_barrier((proto_sum, emb_grad, proto_scale))
    proto_sum = gathered(proto_sum, "y").reshape(slots, width)
    proto_grad = proto_scale * proto_sum.astype(f32)
    return (emb_grad, proto_grad)


def solution(mesh):
    inner = Mesh(mesh.devices.reshape(16, 4, 4, 2), ("z", "y", "x", "core"))
    return jax.shard_map(
        body,
        mesh=inner,
        in_specs=(P(rows_axes, None), P(proto_axes, None), P(rows_axes)),
        out_specs=(P(rows_axes, None), P(proto_axes, None)),
        check_vma=False,
    )
```

```python
import jax
import jax.numpy as jnp
from jax import lax
from jax.experimental import pallas as pl
from jax.experimental.pallas import tpu as pltpu
from jax.sharding import Mesh, PartitionSpec as P

ITERS = 3


epsilon_code = 0.05
sharpness_divisor = 0.1
norm_floor = 1e-06
rows_axes = ("z", "y")
proto_axes = ("x", "core")
LANES = 128
ROWS = 256
f32 = jnp.float32
bf16 = jnp.bfloat16
SENT = jnp.float16
FOLD = 8
LOG2_E = 1.4426950408889634


def shifted(value, axis, steps):
    count = lax.axis_size(axis)
    pairs = [(source, (source + steps) % count) for source in range(count)]
    return lax.ppermute(value, axis, pairs)


def exchanged(value, axis):
    return lax.all_to_all(value, axis, 0, 0, tiled=True)


def gathered(value, axis):
    return exchanged(jnp.broadcast_to(value[None], (lax.axis_size(axis),) + value.shape), axis)


def unit_rows(values):
    wide = values.astype(f32)
    scale = lax.rsqrt(jnp.mean(wide * wide, axis=1, keepdims=True) + norm_floor) / jnp.sqrt(
        f32(wide.shape[1])
    )
    return (wide * scale, scale)


def row_scale(values):
    return unit_rows(values)[1]


def tangent(upstream, units):
    return upstream - units * jnp.sum(units * upstream, axis=1, keepdims=True)


def total(pieces):
    parts = [pieces[index].astype(f32) for index in range(pieces.shape[0])]
    while len(parts) > 1:
        parts = [left + right for left, right in zip(parts[::2], parts[1::2], strict=True)]
    return parts[0]


def block(value, index, count):
    size = value.shape[0] // count
    return lax.dynamic_slice_in_dim(value, index * size, size, 0)


def scatter_sum(value, axis, me):
    count = lax.axis_size(axis)
    total = block(value, me, count).astype(f32)
    for step in range(1, count):
        piece = shifted(block(value, (me + step) % count, count), axis, step)
        total = total + piece.astype(f32)
    return total.astype(value.dtype)


def gather_blocks_early(value, axis, me):
    count = lax.axis_size(axis)
    out = jnp.zeros((count,) + value.shape, value.dtype)
    for step in range(count):
        piece = (shifted(value, axis, step) if step else value)[None]
        out = lax.dynamic_update_slice_in_dim(out, piece, (me + count - step) % count, 0)
    return out.reshape((-1,) + value.shape[1:])


def gather_blocks(value, axis, me):
    count = lax.axis_size(axis)
    out = jnp.broadcast_to(value[None], (count,) + value.shape)
    for step in range(1, count):
        piece = shifted(value, axis, step)[None]
        out = lax.dynamic_update_slice_in_dim(out, piece, (me + count - step) % count, 0)
    return out.reshape((-1,) + value.shape[1:])


def kernel_units(values):
    wide = values.astype(f32)
    mean = jnp.sum(wide * wide, axis=1, keepdims=True) * (1.0 / wide.shape[1])
    scale = lax.rsqrt(mean + norm_floor) * (1.0 / wide.shape[1] ** 0.5)
    return (wide * scale).astype(bf16)


def as_row(partials):
    return jnp.sum(partials.T, axis=0, keepdims=True)


def as_column(row):
    return jnp.broadcast_to(row, (LANES, row.shape[1])).T


def column_tile(values, start):
    width = values.shape[1]
    return values[start // width : start // width + 1, start % width : start % width + LANES]


def add_column(ref, start, values):
    width = ref.shape[2]
    tile = (0, slice(start // width, start // width + 1), slice(start % width, start % width + LANES))
    ref[tile] += jnp.sum(values, axis=0, keepdims=True)


def tiles(matrix):
    return range(0, matrix.shape[1], LANES)


def tempered_rows(units, protos_ref, divisor):
    scores = lax.dot_general(
        units, protos_ref[...], (((1,), (1,)), ((), ())), preferred_element_type=f32
    )
    return jnp.exp2(scores * (LOG2_E / divisor))


def steps(count):
    return [slice(start, start + ROWS) for start in range(0, count, ROWS)]


def for_each_receiver(ref):
    for to in range(1, ref.shape[0]):
        ref[to] = ref[0]


def first_kernel(emb_ref, proto_ref, views_ref, protos_ref, col_ref):
    protos_ref[...] = kernel_units(proto_ref[...])
    views_ref[...] = kernel_units(emb_ref[...])
    col_ref[0] = jnp.zeros_like(col_ref[0])

    @pl.loop(0, emb_ref.shape[0] // ROWS)
    def _(step):
        rows = pl.ds(pl.multiple_of(step * ROWS, ROWS), ROWS)
        tempered = tempered_rows(views_ref[rows, :], protos_ref, sharpness_divisor)
        for start in tiles(tempered):
            value = tempered[:, start : start + LANES]
            add_column(col_ref, start, value * value)

    for_each_receiver(col_ref)


def rows_kernel(views_ref, protos_ref, totals_ref, temp_ref, row_ref):
    column_scale = 1.0 / jnp.sum(totals_ref[...].astype(f32), axis=0)

    @pl.loop(0, views_ref.shape[0] // ROWS)
    def _(step):
        rows = pl.ds(pl.multiple_of(step * ROWS, ROWS), ROWS)
        tempered = tempered_rows(views_ref[rows, :], protos_ref, sharpness_divisor)
        temp_ref[rows, :] = tempered
        total = soft = jnp.zeros((ROWS, LANES), f32)
        for start in tiles(tempered):
            value = tempered[:, start : start + LANES]
            soft = soft + value
            total = total + value * value * column_tile(column_scale, start)
        row_ref[0, :1, rows] = as_row(total)
        row_ref[0, 1:, rows] = as_row(soft)

    for_each_receiver(row_ref)


def line_kernel(views_ref, protos_ref, totals_ref, kernel_ref, row_ref):
    column_scale = 1.0 / jnp.sum(totals_ref[...], axis=0)

    @pl.loop(0, views_ref.shape[0] // ROWS)
    def _(step):
        rows = pl.ds(pl.multiple_of(step * ROWS, ROWS), ROWS)
        kernel = tempered_rows(views_ref[rows, :], protos_ref, epsilon_code)
        kernel_ref[rows, :] = kernel
        total = jnp.zeros((ROWS, LANES), f32)
        for start in tiles(kernel):
            total = total + kernel[:, start : start + LANES] * column_tile(column_scale, start)
        row_ref[0, :, rows] = as_row(total)

    for_each_receiver(row_ref)


def col_kernel(temp_ref, totals_ref, col_ref):
    weight = 1.0 / jnp.sum(totals_ref[:, 0, :], axis=0, keepdims=True)
    col_ref[0] = jnp.zeros_like(col_ref[0])
    for rows in steps(temp_ref.shape[0]):
        wide = as_column(weight[:, rows])
        for start in tiles(temp_ref):
            value = temp_ref[rows, start : start + LANES]
            add_column(col_ref, start, value * value * wide)
    for_each_receiver(col_ref)


def gradient_kernel(
    other_ref, totals_ref, line_ref, soft_ref, views_ref, protos_ref, view_ref, proto_ref
):
    proto_ref[...] = jnp.zeros_like(proto_ref)
    column_scale = 1.0 / jnp.sum(totals_ref[...], axis=0)
    line_row = 1.0 / jnp.sum(line_ref[:, 0, :], axis=0, keepdims=True)
    soft_row = 1.0 / jnp.sum(soft_ref[:, 1, :], axis=0, keepdims=True)
    for rows in steps(other_ref.shape[0]):
        line = as_column(line_row[:, rows])
        soft = as_column(soft_row[:, rows])
        views = views_ref[rows, :]
        tempered = tempered_rows(views, protos_ref, sharpness_divisor)
        grads = []
        for start in tiles(tempered):
            codes = other_ref[rows, start : start + LANES]
            codes = (codes * column_tile(column_scale, start) * line).astype(bf16)
            likelihood = tempered[:, start : start + LANES] * soft
            grads.append(
                ((likelihood - codes.astype(f32)) * (1.0 / sharpness_divisor)).astype(bf16)
            )
        grad = jnp.concatenate(grads, axis=1)
        view_ref[rows, :] = jnp.dot(grad, protos_ref[...], preferred_element_type=f32)
        proto_ref[...] += lax.dot_general(
            grad, views, (((0,), (0,)), ((), ())), preferred_element_type=f32
        )


def call(kernel, name, ins, outs, flops, size, exps=0):
    in_vmem = pl.BlockSpec(memory_space=pltpu.VMEM)
    return pl.pallas_call(
        kernel,
        name=name,
        out_shape=[jax.ShapeDtypeStruct(shape, kind) for shape, kind in outs],
        in_specs=[in_vmem] * len(ins),
        out_specs=[in_vmem] * len(outs),
        compiler_params=pltpu.CompilerParams(vmem_limit_bytes=16 * 2**20),
        cost_estimate=pl.CostEstimate(flops=flops, bytes_accessed=size, transcendentals=exps),
    )(*ins)


def body(embeddings, prototypes, partner):
    count, width = embeddings.shape
    slots = prototypes.shape[0]
    entries = count * slots
    links = jnp.remainder(partner, count)
    y, z, x, core = (lax.axis_index(name) for name in ("y", "z", "x", "core"))
    y_count, z_count, x_count = (lax.axis_size(name) for name in ("y", "z", "x"))
    matrix, column = (count, slots), (FOLD, slots // FOLD)
    members = 2 * x_count
    own = block(embeddings, x * 2 + core, members)
    sent = shifted(own, "z", z_count // 2)
    views, protos, column_part = call(
        first_kernel,
        "first",
        [embeddings, prototypes],
        [((count, width), bf16), ((slots, width), bf16), ((y_count,) + column, f32)],
        flops=2 * entries * width,
        size=4 * slots * width,
        exps=entries,
    )

    def tempered_pass(rows, totals):
        tempered, part = call(
            rows_kernel,
            "tempered_pass",
            [rows, protos, totals],
            [(matrix, f32), ((members, 2, count), f32)],
            flops=2 * entries * width,
            size=4 * slots * width,
            exps=entries,
        )
        return tempered, exchanged(part, proto_axes)

    def column_pass(tempered, totals):
        sums = ((y_count,) + column, f32)
        (part,) = call(col_kernel, "column_pass", [tempered, totals], [sums], 3 * entries, 4 * count)
        return total(exchanged(part, "y"))

    sent = gather_blocks_early(gather_blocks_early(sent, "core", core), "x", x)
    column_part = total(exchanged(column_part, "y"))
    column_total = gathered(column_part.astype(bf16), "z")
    column_total, sent = lax.optimization_barrier((column_total, sent))
    tempered, row_total = tempered_pass(views, column_total)
    column_part, sent = lax.optimization_barrier((column_pass(tempered, row_total), sent))
    other = sent[links]
    column_total = gathered(column_part.astype(bf16), "z")
    for sweep in range(2, ITERS):
        column_total, other, place = lax.optimization_barrier((column_total, other, (y, z, x, core)))
        tempered, row_total = tempered_pass(views, column_total)
        column_part, other = lax.optimization_barrier((column_pass(tempered, row_total), other))
        column_total = gathered(column_part, "z")
    other_views = unit_rows(other)[0].astype(bf16)
    other_kernel, line_part = call(
        line_kernel,
        "lines",
        [other_views, protos, column_total],
        [(matrix, f32), ((members, 1, count), f32)],
        flops=2 * entries * width,
        size=4 * slots * width,
        exps=entries,
    )
    line_total = exchanged(line_part, proto_axes)
    view_part, proto_part = call(
        gradient_kernel,
        "gradient",
        [other_kernel, column_total, line_total, row_total, views, protos],
        [((count, width), f32), ((slots, width), f32)],
        flops=6 * entries * width,
        size=8 * slots * width,
        exps=entries,
    )

    view_part, proto_part, late_emb, late_proto, (y, z, x, core) = lax.optimization_barrier(
        (view_part, proto_part, embeddings, prototypes, place)
    )
    proto_rows = unit_rows(block(late_proto, y * z_count + z, y_count * z_count))[0]
    view_rows = unit_rows(block(late_emb, core * x_count + x, members))[0]
    proto_pieces = exchanged(proto_part.astype(SENT).reshape(y_count, -1, width), "y")
    proto_sum = total(proto_pieces).astype(SENT)
    proto_pieces = exchanged(proto_sum.reshape(z_count, -1, width), "z")
    proto_sum = (tangent(total(proto_pieces), proto_rows) * (1.0 / z_count)).astype(SENT)
    proto_sum = gathered(proto_sum, "z").reshape(-1, width)

    view_sum = scatter_sum(scatter_sum(view_part.astype(SENT), "core", core), "x", x)
    view_sum = tangent(view_sum.astype(f32), view_rows).astype(SENT)
    view_sum = gather_blocks(gather_blocks(view_sum, "x", x), "core", core)

    emb_grad = row_scale(late_emb) * view_sum.astype(f32)
    proto_scale = row_scale(late_proto) * float(z_count)

    proto_sum, emb_grad, proto_scale = lax.optimization_barrier((proto_sum, emb_grad, proto_scale))
    proto_sum = gathered(proto_sum, "y").reshape(slots, width)
    proto_grad = proto_scale * proto_sum.astype(f32)
    return (emb_grad, proto_grad)


def solution(mesh):
    inner = Mesh(mesh.devices.reshape(16, 4, 4, 2), ("z", "y", "x", "core"))
    return jax.shard_map(
        body,
        mesh=inner,
        in_specs=(P(rows_axes, None), P(proto_axes, None), P(rows_axes)),
        out_specs=(P(rows_axes, None), P(proto_axes, None)),
        check_vma=False,
    )
```

```python
import jax
import jax.numpy as jnp
from jax import lax
from jax.experimental import pallas as pl
from jax.experimental.pallas import tpu as pltpu
from jax.sharding import Mesh, PartitionSpec as P

ITERS = 3


epsilon_code = 0.05
sharpness_divisor = 0.1
norm_floor = 1e-06
rows_axes = ("z", "y")
proto_axes = ("x", "core")
LANES = 128
ROWS = 256
f32 = jnp.float32
bf16 = jnp.bfloat16
SENT = jnp.float16
FOLD = 8
LOG2_E = 1.4426950408889634


def shifted(value, axis, steps):
    count = lax.axis_size(axis)
    pairs = [(source, (source + steps) % count) for source in range(count)]
    return lax.ppermute(value, axis, pairs)


def exchanged(value, axis):
    return lax.all_to_all(value, axis, 0, 0, tiled=True)


def gathered(value, axis):
    return exchanged(jnp.broadcast_to(value[None], (lax.axis_size(axis),) + value.shape), axis)


def unit_rows(values):
    wide = values.astype(f32)
    scale = lax.rsqrt(jnp.mean(wide * wide, axis=1, keepdims=True) + norm_floor) / jnp.sqrt(
        f32(wide.shape[1])
    )
    return (wide * scale, scale)


def row_scale(values):
    return unit_rows(values)[1]


def tangent(upstream, units):
    return upstream - units * jnp.sum(units * upstream, axis=1, keepdims=True)


def total(pieces):
    parts = [pieces[index].astype(f32) for index in range(pieces.shape[0])]
    while len(parts) > 1:
        parts = [left + right for left, right in zip(parts[::2], parts[1::2], strict=True)]
    return parts[0]


def block(value, index, count):
    size = value.shape[0] // count
    return lax.dynamic_slice_in_dim(value, index * size, size, 0)


def scatter_sum(value, axis, me):
    count = lax.axis_size(axis)
    total = block(value, me, count).astype(f32)
    for step in range(1, count):
        piece = shifted(block(value, (me + step) % count, count), axis, step)
        total = total + piece.astype(f32)
    return total.astype(value.dtype)


def gather_blocks_early(value, axis, me):
    count = lax.axis_size(axis)
    out = jnp.zeros((count,) + value.shape, value.dtype)
    for step in range(count):
        piece = (shifted(value, axis, step) if step else value)[None]
        out = lax.dynamic_update_slice_in_dim(out, piece, (me + count - step) % count, 0)
    return out.reshape((-1,) + value.shape[1:])


def gather_blocks(value, axis, me):
    count = lax.axis_size(axis)
    out = jnp.broadcast_to(value[None], (count,) + value.shape)
    for step in range(1, count):
        piece = shifted(value, axis, step)[None]
        out = lax.dynamic_update_slice_in_dim(out, piece, (me + count - step) % count, 0)
    return out.reshape((-1,) + value.shape[1:])


def kernel_units(values):
    wide = values.astype(f32)
    mean = jnp.sum(wide * wide, axis=1, keepdims=True) * (1.0 / wide.shape[1])
    scale = lax.rsqrt(mean + norm_floor) * (1.0 / wide.shape[1] ** 0.5)
    return (wide * scale).astype(bf16)


def as_row(partials):
    return jnp.sum(partials.T, axis=0, keepdims=True)


def as_column(row):
    return jnp.broadcast_to(row, (LANES, row.shape[1])).T


def column_tile(values, start):
    width = values.shape[1]
    return values[start // width : start // width + 1, start % width : start % width + LANES]


def add_column(ref, start, values):
    width = ref.shape[2]
    tile = (0, slice(start // width, start // width + 1), slice(start % width, start % width + LANES))
    ref[tile] += jnp.sum(values, axis=0, keepdims=True)


def tiles(matrix):
    return range(0, matrix.shape[1], LANES)


def tempered_rows(units, protos_ref, divisor):
    scores = lax.dot_general(
        units, protos_ref[...], (((1,), (1,)), ((), ())), preferred_element_type=f32
    )
    return jnp.exp2(scores * (LOG2_E / divisor))


def steps(count):
    return [slice(start, start + ROWS) for start in range(0, count, ROWS)]


def for_each_receiver(ref):
    for to in range(1, ref.shape[0]):
        ref[to] = ref[0]


def first_kernel(emb_ref, proto_ref, views_ref, protos_ref, col_ref):
    protos_ref[...] = kernel_units(proto_ref[...])
    views_ref[...] = kernel_units(emb_ref[...])
    col_ref[0] = jnp.zeros_like(col_ref[0])

    @pl.loop(0, emb_ref.shape[0] // ROWS)
    def _(step):
        rows = pl.ds(pl.multiple_of(step * ROWS, ROWS), ROWS)
        tempered = tempered_rows(views_ref[rows, :], protos_ref, sharpness_divisor)
        for start in tiles(tempered):
            value = tempered[:, start : start + LANES]
            add_column(col_ref, start, value * value)

    for_each_receiver(col_ref)


def rows_kernel(views_ref, protos_ref, totals_ref, temp_ref, row_ref):
    column_scale = 1.0 / jnp.sum(totals_ref[...].astype(f32), axis=0)

    @pl.loop(0, views_ref.shape[0] // ROWS)
    def _(step):
        rows = pl.ds(pl.multiple_of(step * ROWS, ROWS), ROWS)
        tempered = tempered_rows(views_ref[rows, :], protos_ref, sharpness_divisor)
        temp_ref[rows, :] = tempered
        total = soft = jnp.zeros((ROWS, LANES), f32)
        for start in tiles(tempered):
            value = tempered[:, start : start + LANES]
            soft = soft + value
            total = total + value * value * column_tile(column_scale, start)
        row_ref[0, :1, rows] = as_row(total)
        row_ref[0, 1:, rows] = as_row(soft)

    for_each_receiver(row_ref)


def line_kernel(views_ref, protos_ref, totals_ref, kernel_ref, row_ref):
    column_scale = 1.0 / jnp.sum(totals_ref[...], axis=0)

    @pl.loop(0, views_ref.shape[0] // ROWS)
    def _(step):
        rows = pl.ds(pl.multiple_of(step * ROWS, ROWS), ROWS)
        kernel = tempered_rows(views_ref[rows, :], protos_ref, epsilon_code)
        kernel_ref[rows, :] = kernel
        total = jnp.zeros((ROWS, LANES), f32)
        for start in tiles(kernel):
            total = total + kernel[:, start : start + LANES] * column_tile(column_scale, start)
        row_ref[0, :, rows] = as_row(total)

    for_each_receiver(row_ref)


def col_kernel(temp_ref, totals_ref, col_ref):
    weight = 1.0 / jnp.sum(totals_ref[:, 0, :], axis=0, keepdims=True)
    col_ref[0] = jnp.zeros_like(col_ref[0])
    for rows in steps(temp_ref.shape[0]):
        wide = as_column(weight[:, rows])
        for start in tiles(temp_ref):
            value = temp_ref[rows, start : start + LANES]
            add_column(col_ref, start, value * value * wide)
    for_each_receiver(col_ref)


def gradient_kernel(
    other_ref, totals_ref, line_ref, soft_ref, views_ref, protos_ref, view_ref, proto_ref
):
    proto_ref[...] = jnp.zeros_like(proto_ref)
    column_scale = 1.0 / jnp.sum(totals_ref[...], axis=0)
    line_row = 1.0 / jnp.sum(line_ref[:, 0, :], axis=0, keepdims=True)
    soft_row = 1.0 / jnp.sum(soft_ref[:, 1, :], axis=0, keepdims=True)
    for rows in steps(other_ref.shape[0]):
        line = as_column(line_row[:, rows])
        soft = as_column(soft_row[:, rows])
        views = views_ref[rows, :]
        tempered = tempered_rows(views, protos_ref, sharpness_divisor)
        grads = []
        for start in tiles(tempered):
            codes = other_ref[rows, start : start + LANES]
            codes = (codes * column_tile(column_scale, start) * line).astype(bf16)
            likelihood = tempered[:, start : start + LANES] * soft
            grads.append(
                ((likelihood - codes.astype(f32)) * (1.0 / sharpness_divisor)).astype(bf16)
            )
        grad = jnp.concatenate(grads, axis=1)
        view_ref[rows, :] = jnp.dot(grad, protos_ref[...], preferred_element_type=f32)
        proto_ref[...] += lax.dot_general(
            grad, views, (((0,), (0,)), ((), ())), preferred_element_type=f32
        )


def call(kernel, name, ins, outs, flops, size, exps=0):
    in_vmem = pl.BlockSpec(memory_space=pltpu.VMEM)
    return pl.pallas_call(
        kernel,
        name=name,
        out_shape=[jax.ShapeDtypeStruct(shape, kind) for shape, kind in outs],
        in_specs=[in_vmem] * len(ins),
        out_specs=[in_vmem] * len(outs),
        compiler_params=pltpu.CompilerParams(vmem_limit_bytes=16 * 2**20),
        cost_estimate=pl.CostEstimate(flops=flops, bytes_accessed=size, transcendentals=exps),
    )(*ins)


def body(embeddings, prototypes, partner):
    count, width = embeddings.shape
    slots = prototypes.shape[0]
    entries = count * slots
    links = jnp.remainder(partner, count)
    y, z, x, core = (lax.axis_index(name) for name in ("y", "z", "x", "core"))
    y_count, z_count, x_count = (lax.axis_size(name) for name in ("y", "z", "x"))
    matrix, column = (count, slots), (FOLD, slots // FOLD)
    members = 2 * x_count
    own = block(embeddings, x * 2 + core, members)
    sent = shifted(own, "z", z_count // 2)
    views, protos, column_part = call(
        first_kernel,
        "first",
        [embeddings, prototypes],
        [((count, width), bf16), ((slots, width), bf16), ((y_count,) + column, f32)],
        flops=2 * entries * width,
        size=4 * slots * width,
        exps=entries,
    )

    def tempered_pass(rows, totals):
        tempered, part = call(
            rows_kernel,
            "tempered_pass",
            [rows, protos, totals],
            [(matrix, f32), ((members, 2, count), f32)],
            flops=2 * entries * width,
            size=4 * slots * width,
            exps=entries,
        )
        return tempered, exchanged(part, proto_axes)

    def column_pass(tempered, totals):
        sums = ((y_count,) + column, f32)
        (part,) = call(col_kernel, "column_pass", [tempered, totals], [sums], 3 * entries, 4 * count)
        return total(exchanged(part, "y"))

    sent = gather_blocks_early(gather_blocks_early(sent, "core", core), "x", x)
    column_part = total(exchanged(column_part, "y"))
    column_total = gathered(column_part.astype(bf16), "z")
    column_total, sent = lax.optimization_barrier((column_total, sent))
    tempered, row_total = tempered_pass(views, column_total)
    column_part, sent = lax.optimization_barrier((column_pass(tempered, row_total), sent))
    other = sent[links]
    column_total = gathered(column_part.astype(bf16), "z")
    for sweep in range(2, ITERS):
        column_total, other, place = lax.optimization_barrier((column_total, other, (y, z, x, core)))
        tempered, row_total = tempered_pass(views, column_total)
        column_part, other = lax.optimization_barrier((column_pass(tempered, row_total), other))
        column_total = gathered(column_part, "z")
    other_views = unit_rows(other)[0].astype(bf16)
    other_kernel, line_part = call(
        line_kernel,
        "lines",
        [other_views, protos, column_total],
        [(matrix, f32), ((members, 1, count), f32)],
        flops=2 * entries * width,
        size=4 * slots * width,
        exps=entries,
    )
    line_total = exchanged(line_part, proto_axes)
    view_part, proto_part = call(
        gradient_kernel,
        "gradient",
        [other_kernel, column_total, line_total, row_total, views, protos],
        [((count, width), f32), ((slots, width), f32)],
        flops=6 * entries * width,
        size=8 * slots * width,
        exps=entries,
    )

    view_part, proto_part, late_emb, late_proto, (y, z, x, core) = lax.optimization_barrier(
        (view_part.astype(SENT), proto_part, embeddings, prototypes, place)
    )
    proto_rows = unit_rows(block(late_proto, y * z_count + z, y_count * z_count))[0]
    view_rows = unit_rows(block(late_emb, core * x_count + x, members))[0]
    proto_pieces = exchanged(proto_part.astype(SENT).reshape(y_count, -1, width), "y")
    proto_sum = total(proto_pieces).astype(SENT)
    proto_pieces = exchanged(proto_sum.reshape(z_count, -1, width), "z")
    proto_sum = (tangent(total(proto_pieces), proto_rows) * (1.0 / z_count)).astype(SENT)
    proto_sum = gathered(proto_sum, "z").reshape(-1, width)

    view_sum = scatter_sum(scatter_sum(view_part, "core", core), "x", x)
    view_sum = tangent(view_sum.astype(f32), view_rows).astype(SENT)
    view_sum = gather_blocks(gather_blocks(view_sum, "x", x), "core", core)

    emb_grad = row_scale(late_emb) * view_sum.astype(f32)
    proto_scale = row_scale(late_proto) * float(z_count)

    proto_sum, emb_grad, proto_scale = lax.optimization_barrier((proto_sum, emb_grad, proto_scale))
    proto_sum = gathered(proto_sum, "y").reshape(slots, width)
    proto_grad = proto_scale * proto_sum.astype(f32)
    return (emb_grad, proto_grad)


def solution(mesh):
    inner = Mesh(mesh.devices.reshape(16, 4, 4, 2), ("z", "y", "x", "core"))
    return jax.shard_map(
        body,
        mesh=inner,
        in_specs=(P(rows_axes, None), P(proto_axes, None), P(rows_axes)),
        out_specs=(P(rows_axes, None), P(proto_axes, None)),
        check_vma=False,
    )
```
